32 devices in a mesh: noise: 8 (over z, y), tile: 4 (over x, core).
Axes of the slice: x: 2, y: 2, z: 4, core: 2. Of those that a mesh axis runs over, the one named last changes fastest.
Arguments:
- queue_state: float32 [32, 69, 4, 256], P('noise', None, 'tile'), may hold values from -6 to 6
- fresh_noise: float32 [2, 69, 4, 256], P(None, None, 'tile'), may hold values from -6 to 6
- plan: float32 [17], replicated, may hold values from 0.5 to 2
- levels: int32 [32], P('noise'), may hold values from 0 to 15
- neighbours: int32 [4, 4], replicated, may hold values from -1 to 3, as said below
- in_weight: bfloat16 [256, 69], replicated, may hold values from -0.75 to 0.75
- level_embed: float32 [256], replicated, may hold values from -3 to 3
- conv_weight: bfloat16 [9, 256, 256], replicated, may hold values from -0.125 to 0.125
- norm_gain: float32 [256], replicated, may hold values from 0.5 to 1.5
- query_weight: bfloat16 [256, 256], replicated, may hold values from -0.375 to 0.375
- memory_weight: bfloat16 [512, 256], replicated, may hold values from -0.375 to 0.375
- attend_out: bfloat16 [256, 256], replicated, may hold values from -0.375 to 0.375
- decode_weight: bfloat16 [69, 256], replicated, may hold values from -0.375 to 0.375
Outputs:
- queue_after: float32 [32, 69, 4, 256], P('noise', None, 'tile')
The draws below stay inside these ranges and needn't reach their ends.
Inputs may be any that keep to these rules, and one draw needn't show every extreme that they name: The tiles fill a grid of 2 rows and 2 columns, each tile once, in an arrangement drawn per run; west and east neighbours run along a row, which closes into a loop; -1 stands for the missing north neighbour of the first row and south neighbour of the last row.
All inputs are finite; a program needn't handle non-finite values.
Results may differ from the reference program's by a relative error of at most 0.012.
Values may be sent and summed in bfloat16 or wider, within the bound.
A program may use at most 64 MiB of HBM per device.

```python
import math
import jax
import jax.numpy as jnp
from jax import lax

FIELDS = 69
WIDTH = 256
HEADS = 8
TILE = 16
FR_DEV = 4
LEVELS = 16
STEPS = 2
TILE_ROWS = 2
NTILES = 4
QUEUE = 32


def place_tile(placed, slot_index, tile_id):
    where_now = jnp.argmax((placed == tile_id).astype(jnp.int32)).astype(jnp.int32)
    held = placed[slot_index]
    placed = placed.at[where_now].set(held)
    return placed.at[slot_index].set(tile_id)


def draw_neighbours(key, part):
    column_count = NTILES // TILE_ROWS
    half_away = NTILES // 2
    order_key = jax.random.fold_in(key, 11)
    anchor_key = jax.random.fold_in(key, 12)
    column_key = jax.random.fold_in(key, 13)
    row_key = jax.random.fold_in(key, 14)
    placed = jax.random.permutation(order_key, NTILES).astype(jnp.int32)
    anchor = jax.random.randint(anchor_key, (), 0, NTILES).astype(jnp.int32)
    anchor_col = jax.random.randint(column_key, (), 0, column_count).astype(jnp.int32)
    anchor_row = jax.random.randint(row_key, (), 0, 2).astype(jnp.int32)
    other_row = (1 - anchor_row).astype(jnp.int32)
    first_slot = (anchor_row * column_count + anchor_col).astype(jnp.int32)
    east_slot = (anchor_row * column_count + (anchor_col + 1) % column_count).astype(jnp.int32)
    below_slot = (other_row * column_count + anchor_col).astype(jnp.int32)
    placed = place_tile(placed, first_slot, anchor)
    placed = place_tile(placed, east_slot, ((anchor + half_away) % NTILES).astype(jnp.int32))
    placed = place_tile(placed, below_slot, ((anchor + 1) % NTILES).astype(jnp.int32))
    where_is = jnp.argsort(placed, stable=True).astype(jnp.int32)
    row_of = where_is // column_count
    column_of = where_is % column_count
    west_tile = placed[row_of * column_count + (column_of + column_count - 1) % column_count]
    east_tile = placed[row_of * column_count + (column_of + 1) % column_count]
    north_tile = jnp.where(row_of > 0, placed[jnp.maximum(row_of - 1, 0) * column_count + column_of], -1)
    south_tile = jnp.where(row_of < TILE_ROWS - 1, placed[jnp.minimum(row_of + 1, TILE_ROWS - 1) * column_count + column_of], -1)
    return jnp.stack([west_tile, east_tile, north_tile, south_tile], axis=1).astype(jnp.int32)


def set_ends(entries, rng, smallest, high):
    longest = entries.shape.index(max(entries.shape))
    spots = []
    for shift in (0, 1):
        where = [jax.random.randint(jax.random.fold_in(rng, axis), (), 0, length) for axis, length in enumerate(entries.shape)]
        where[longest] = (where[longest] + shift) % entries.shape[longest]
        spots.append(tuple(where))
    return entries.at[spots[0]].set(smallest).at[spots[1]].set(high)


def block_scale(own_key, shape, cuts, smallest, top_value):
    loudness = 1.0
    for axis_at, shards_of in cuts:
        draws = jax.random.uniform(jax.random.fold_in(jax.random.fold_in(own_key, 6), axis_at), (shards_of,), jnp.float32, smallest / len(cuts), top_value / len(cuts))
        loudness = loudness * jnp.repeat(jnp.exp(draws), shape[axis_at] // shards_of).reshape((-1,) + (1,) * (len(shape) - 1 - axis_at))
    return loudness


def centred(stream_key, shape, deviation, most, pieces=(), kind=jnp.bfloat16):
    result = jax.random.normal(stream_key, shape, jnp.float32) * deviation
    if len(pieces) > 0:
        result = block_scale(stream_key, shape, pieces, -0.22, 0.18) * result
    return jnp.clip(result, min=-most, max=most).astype(kind)


def setup_inputs(seed: int = 0) -> dict:
    keys = jax.random.split(jax.random.key(seed), 14)
    queue_state = centred(keys[0], (QUEUE, FIELDS, NTILES, TILE * TILE), 1.0, 6.0, ((0, 8), (2, 4)), jnp.float32)
    fresh_noise = centred(keys[1], (STEPS, FIELDS, NTILES, TILE * TILE), 1.0, 6.0, ((2, 4),), jnp.float32)
    plan = jnp.clip(jnp.exp(jax.random.uniform(keys[2], (LEVELS + 1,), jnp.float32, math.log(0.5), math.log(2.0))), 0.5, 2.0)
    levels = set_ends(jax.random.randint(keys[3], (QUEUE,), 0, LEVELS), jax.random.fold_in(keys[3], 1), 0, LEVELS - 1).astype(jnp.int32)
    neighbours = draw_neighbours(jax.random.fold_in(keys[13], 71), 0)
    in_weight = centred(keys[5], (WIDTH, FIELDS), FIELDS ** -0.5, 0.75)
    level_embed = centred(keys[6], (WIDTH,), 0.5, 3.0, (), jnp.float32)
    conv_weight = centred(keys[7], (9, WIDTH, WIDTH), (9 * WIDTH) ** -0.5, 0.125)
    norm_gain = jnp.clip(1.0 + 0.1 * jax.random.normal(keys[8], (WIDTH,), jnp.float32), 0.5, 1.5)
    query_weight = centred(keys[9], (WIDTH, WIDTH), WIDTH ** -0.5, 0.375)
    memory_weight = centred(keys[10], (2 * WIDTH, WIDTH), WIDTH ** -0.5, 0.375)
    attend_out = centred(keys[11], (WIDTH, WIDTH), WIDTH ** -0.5, 0.375)
    decode_weight = centred(keys[12], (FIELDS, WIDTH), WIDTH ** -0.5, 0.375)
    return {"queue_state": queue_state, "fresh_noise": fresh_noise, "plan": plan, "levels": levels, "neighbours": neighbours, "in_weight": in_weight, "level_embed": level_embed, "conv_weight": conv_weight, "norm_gain": norm_gain, "query_weight": query_weight, "memory_weight": memory_weight, "attend_out": attend_out, "decode_weight": decode_weight}


def pick_tiles(source, tile_index):
    chosen = jnp.take(source, jnp.maximum(tile_index, 0), axis=1)
    return jnp.where((tile_index >= 0)[None, :, None], chosen, jnp.zeros_like(chosen))

def pad_tiles(frame_low, neighbours):
    west_col = pick_tiles(frame_low[:, :, :, TILE - 1], neighbours[:, 0])
    east_col = pick_tiles(frame_low[:, :, :, 0], neighbours[:, 1])
    middle = jnp.concatenate([west_col[..., None], frame_low, east_col[..., None]], axis=3)
    north_row = pick_tiles(middle[:, :, TILE - 1, :], neighbours[:, 2])
    south_row = pick_tiles(middle[:, :, 0, :], neighbours[:, 3])
    return jnp.concatenate([north_row[:, :, None, :], middle, south_row[:, :, None, :]], axis=2)

def frame_features(frame_state, sigma_one, in_weight, level_embed, conv_weight, norm_gain, neighbours):
    cell_count = NTILES * TILE * TILE
    in_scale = 1.0 / jnp.sqrt(sigma_one * sigma_one + 1.0)
    scaled = (in_scale * frame_state).reshape(FIELDS, cell_count).astype(jnp.bfloat16)
    lifted = jnp.dot(in_weight, scaled, preferred_element_type=jnp.float32) + jnp.log(sigma_one) * level_embed[:, None]
    lifted_low = lax.optimization_barrier(lifted.astype(jnp.bfloat16))
    padded = pad_tiles(lifted_low.reshape(WIDTH, NTILES, TILE, TILE), neighbours)
    convolved = jnp.zeros((WIDTH, cell_count), jnp.float32)
    for offset in range(9):
        down_by = offset // 3
        right_by = offset % 3
        window = padded[:, :, down_by:down_by + TILE, right_by:right_by + TILE].reshape(WIDTH, cell_count)
        convolved = convolved + jnp.dot(conv_weight[offset], window, preferred_element_type=jnp.float32)
    hidden = lax.optimization_barrier((lifted_low.astype(jnp.float32) + jax.nn.silu(convolved)).astype(jnp.bfloat16))
    widened = hidden.astype(jnp.float32)
    normed = (widened * lax.rsqrt(lax.optimization_barrier(jnp.mean(widened * widened, axis=0, keepdims=True)) + 1e-06) * norm_gain[:, None]).astype(jnp.bfloat16)
    return (hidden, normed)

def denoise(queue_now, sigmas, sigmas_next, neighbours, in_weight, level_embed, conv_weight, norm_gain, query_weight, memory_weight, attend_out, decode_weight):
    cell_count = NTILES * TILE * TILE
    head_size = WIDTH // HEADS

    def per_frame(frame_pair):
        frame_state, sigma_one = frame_pair
        hidden, normed = frame_features(frame_state, sigma_one, in_weight, level_embed, conv_weight, norm_gain, neighbours)
        queries = jnp.dot(query_weight, normed, preferred_element_type=jnp.float32).astype(jnp.bfloat16)
        memory = jnp.dot(memory_weight, normed, preferred_element_type=jnp.float32).astype(jnp.bfloat16)
        return (hidden, queries, memory)
    hidden_all, queries_all, memory_all = lax.map(per_frame, (queue_now, sigmas))
    memory_all = jnp.concatenate([memory_all, jnp.zeros((FR_DEV,) + memory_all.shape[1:], memory_all.dtype)], axis=0)

    def per_block(block_id):
        begin_at = (block_id * FR_DEV).astype(jnp.int32)
        block_query = lax.dynamic_slice_in_dim(queries_all, begin_at, FR_DEV, 0).astype(jnp.float32)
        block_query = block_query.reshape(FR_DEV, HEADS, head_size, cell_count)
        block_memory = lax.dynamic_slice_in_dim(memory_all, begin_at, 2 * FR_DEV, 0).astype(jnp.float32)
        key_heads = block_memory[:, :WIDTH].reshape(2 * FR_DEV, HEADS, head_size, cell_count)
        value_heads = block_memory[:, WIDTH:].reshape(2 * FR_DEV, HEADS, head_size, cell_count)
        scores = jnp.einsum('ihdm,jhdm->ijhm', block_query, key_heads, precision=lax.Precision.HIGHEST) * head_size ** (-0.5)
        usable = begin_at + jnp.arange(2 * FR_DEV, dtype=jnp.int32) < QUEUE
        scores = jnp.where(usable[None, :, None, None], scores, -jnp.inf)
        weights = lax.optimization_barrier(jax.nn.softmax(scores, axis=1).astype(jnp.bfloat16)).astype(jnp.float32)
        context = jnp.einsum('ijhm,jhdm->ihdm', weights, value_heads, precision=lax.Precision.HIGHEST)
        context = lax.optimization_barrier(context.astype(jnp.bfloat16)).astype(jnp.float32).reshape(FR_DEV, WIDTH, cell_count)
        attended = jnp.einsum('oc,icm->iom', attend_out.astype(jnp.float32), context, precision=lax.Precision.HIGHEST)
        block_hidden = lax.dynamic_slice_in_dim(hidden_all, begin_at, FR_DEV, 0).astype(jnp.float32)
        refined = lax.optimization_barrier((block_hidden + attended).astype(jnp.bfloat16)).astype(jnp.float32)
        projected = jnp.einsum('fc,icm->ifm', decode_weight.astype(jnp.float32), refined, precision=lax.Precision.HIGHEST)
        block_state = lax.dynamic_slice_in_dim(queue_now, begin_at, FR_DEV, 0).reshape(FR_DEV, FIELDS, cell_count)
        block_sigma = lax.dynamic_slice_in_dim(sigmas, begin_at, FR_DEV, 0)
        block_next = lax.dynamic_slice_in_dim(sigmas_next, begin_at, FR_DEV, 0)
        spread = block_sigma * block_sigma + 1.0
        denoised = (1.0 / spread)[:, None, None] * block_state + (block_sigma / jnp.sqrt(spread))[:, None, None] * projected
        return block_state + ((block_next - block_sigma) / block_sigma)[:, None, None] * (block_state - denoised)
    blocks = lax.map(per_block, jnp.arange(QUEUE // FR_DEV, dtype=jnp.int32))
    return blocks.reshape(queue_now.shape)

def reference(queue_state, fresh_noise, plan, levels, neighbours, in_weight, level_embed, conv_weight, norm_gain, query_weight, memory_weight, attend_out, decode_weight):
    sigmas = plan[levels]
    sigmas_next = plan[levels + 1]
    queue_now = queue_state
    for step_index in range(STEPS):
        entering = sigmas[QUEUE - 1] * fresh_noise[step_index]
        queue_now = jnp.concatenate([queue_now[1:], entering[None]], axis=0)
        queue_now = denoise(queue_now, sigmas, sigmas_next, neighbours, in_weight, level_embed, conv_weight, norm_gain, query_weight, memory_weight, attend_out, decode_weight)
    return queue_now
```

```python
import functools
import math

import jax
import jax.numpy as jnp
from jax import lax
from jax.experimental import pallas as pl
from jax.experimental.pallas import tpu as pltpu
from jax.sharding import PartitionSpec as P

HEADS = 8
MESH = pl.DeviceIdType.MESH
BF = jnp.bfloat16
F32 = jnp.float32


def dot_t(left, right):
    return lax.dot_general(left, right, (((1,), (1,)), ((), ())), preferred_element_type=F32)


def dot_n(left, right):
    return lax.dot_general(left, right, (((1,), (0,)), ((), ())), preferred_element_type=F32)


def kernel(
    groups, tiles, levels, plan, neighbours, queue, noise_rows, in_weight, level_embed, conv_hbm,
    norm_gain, query_raw, memory_raw, attend_raw, decode_weight, out,
    conv_weight, query_weight, memory_weight, attend_out, noise, frames_f32, own_low, next_low, second_low,
    packs, own_edges, next_edges, second_edges, noise_packs, noise_edges, pick,
    sigma_own, sigma_next, lift_weight, head_sum, head_spread, scaled,
    padded, hidden, normed, queries, memory, load_sem,
    own_send, own_recv, next_send, next_recv, body_send, body_recv, second_send, second_recv,
    noise_send, noise_recv, single_send, single_recv,
):
    frame_count, fields, cells = padded.shape[0] // 2, in_weight.shape[0], hidden.shape[1]
    steps = own_low.shape[0]
    width = in_weight.shape[1]
    halves = cells // 128
    side = math.isqrt(cells)
    slots = 2 * side
    head_size = width // HEADS
    reach = 2 * frame_count
    me = lax.axis_index("tile")
    group = lax.axis_index("noise")
    is_last = group == groups - 1
    is_tail = group == groups - 2

    def tile_at(k):
        return lax.rem(me + k, tiles)

    load = pltpu.make_async_copy(conv_hbm, conv_weight, load_sem)
    load.start()
    barrier = pltpu.get_barrier_semaphore()
    for k in range(1, tiles):
        pl.semaphore_signal(
            barrier, 1, device_id={"noise": group, "tile": tile_at(k)}, device_id_type=MESH
        )
    for away in (1, 2):
        @pl.when(group + away < groups)
        def _():
            for k in range(tiles):
                pl.semaphore_signal(
                    barrier, 1, device_id={"noise": group + away, "tile": tile_at(k)},
                    device_id_type=MESH,
                )

    def vertical(tile):
        north = neighbours[tile, 2]
        return north >= 0, jnp.maximum(jnp.where(north >= 0, north, neighbours[tile, 3]), 0)

    place = lax.broadcasted_iota(jnp.int32, (slots, cells), 0)
    cell = lax.broadcasted_iota(jnp.int32, (slots, cells), 1)
    for k in range(1, tiles):
        other = tile_at(k)
        up, above = vertical(other)
        base = jnp.where(up, (side - 1) * side, 0)
        target = jnp.where(
            jnp.logical_and(place == side, neighbours[above, 0] == me), base + side - 1,
            jnp.where(jnp.logical_and(place == side + 1, neighbours[above, 1] == me), base, -1))
        target = jnp.where(
            jnp.logical_and(place < side, above == me), base + place, target)
        target = jnp.where(
            jnp.logical_and(place >= side, neighbours[other, 1] == me), (place - side) * side, target)
        target = jnp.where(
            jnp.logical_and(place < side, neighbours[other, 0] == me), place * side + side - 1, target)
        pick[(k - 1) * slots : k * slots] = jnp.where(cell == target, 1.0, 0.0).astype(BF)

    pairs = frame_count * frame_count
    source = lax.broadcasted_iota(jnp.int32, (pairs * 128, 128), 0)
    target = lax.broadcasted_iota(jnp.int32, (pairs * 128, 128), 1)
    low = source % 128
    combo = source // 128
    head_sum[...] = jnp.where(target == combo * HEADS + low % HEADS, 1.0, 0.0).astype(BF)
    source = lax.broadcasted_iota(jnp.int32, (128, pairs * 128), 0)
    target = lax.broadcasted_iota(jnp.int32, (128, pairs * 128), 1)
    place = target // 128
    combo = place % frame_count * frame_count + place // frame_count
    head_spread[...] = jnp.where(source == combo * HEADS + target % HEADS, 1.0, 0.0).astype(BF)
    source = lax.broadcasted_iota(jnp.int32, (width, width), 1)
    target = lax.broadcasted_iota(jnp.int32, (width, width), 0)
    order = jnp.where(
        source == target % HEADS * head_size + target // HEADS, 1.0, 0.0
    ).astype(BF)
    lift_weight[...] = jnp.zeros_like(lift_weight)
    lift_weight[:fields] = in_weight[...]
    scaled[...] = jnp.zeros_like(scaled)
    packs[...] = jnp.zeros_like(packs)
    noise_packs[...] = jnp.zeros_like(noise_packs)
    sigma_own[...] = jnp.ones_like(sigma_own)
    deltas = []
    for i in range(frame_count):
        sigma_own[i : i + 1] = jnp.full((1, 256), plan[levels[i]], F32)
        deltas.append(jnp.full((1, 256), plan[levels[i] + 1], F32))

    @pl.when(is_last)
    def _():
        sigma_next[...] = jnp.ones_like(sigma_next)
        next_low[...] = jnp.zeros_like(next_low)
        next_edges[...] = jnp.zeros_like(next_edges)

    @pl.when(group >= groups - 2)
    def _():
        second_low[...] = jnp.zeros_like(second_low)
        second_edges[...] = jnp.zeros_like(second_edges)

    for half in range(halves):
        across = slice(half * 128, (half + 1) * 128)
        for i in range(frame_count):
            frames_f32[i, :, across] = queue[pl.ds(i * halves * fields + half, fields, halves), :]
        for i in range(steps):
            noise[i, :, across] = noise_rows[i, :, 0, across]

    west, east = jnp.maximum(neighbours[me, 0], 0), jnp.maximum(neighbours[me, 1], 0)
    has_north, above = vertical(me)
    above_west = jnp.maximum(neighbours[above, 0], 0)
    above_east = jnp.maximum(neighbours[above, 1], 0)

    def copy(source, target_ref, send, recv, where):
        return pltpu.make_async_remote_copy(
            src_ref=source, dst_ref=target_ref, send_sem=send, recv_sem=recv,
            device_id=where, device_id_type=MESH,
        )

    own_parts = [[(1, frame_count)]] + [[(f, f + 1) for f in range(1, frame_count)]] * (steps - 1)
    next_parts = [[(0, 1), (1, frame_count)]] + [[(f, f + 1) for f in range(frame_count)]] * (steps - 1)

    def to_own(step, part, k, sender):
        a, b = part
        return copy(
            packs.at[step, k - 1, a:b], own_edges.at[step, sender, a:b], own_send.at[step, a, k - 1],
            own_recv.at[step, a, sender], {"noise": group, "tile": tile_at(k)},
        )

    def to_next(step, part, k, sender):
        a, b = part
        return copy(
            packs.at[step, k - 1, a:b], next_edges.at[step, sender, a:b], next_send.at[step, a, k - 1],
            next_recv.at[step, a, sender], {"noise": group - 1, "tile": tile_at(k)},
        )

    def body(step, part):
        a, b = part
        return copy(
            own_low.at[step, a:b], next_low.at[step, a:b], body_send.at[step, a], body_recv.at[step, a],
            {"noise": group - 1, "tile": me},
        )

    def to_second(step, k, sender):
        return copy(
            packs.at[step, k - 1, 0], second_edges.at[step, sender], second_send.at[step, k - 1],
            second_recv.at[step, sender], {"noise": group - 2, "tile": tile_at(k)},
        )

    def front(step):
        return copy(
            own_low.at[step, 0], second_low.at[step], single_send.at[1 + step], single_recv.at[1 + step],
            {"noise": group - 2, "tile": me},
        )

    def sigma_copy():
        return copy(
            sigma_own, sigma_next, single_send.at[0], single_recv.at[0],
            {"noise": group - 1, "tile": me},
        )

    def to_noise(k, sender):
        return copy(
            noise_packs.at[k - 1], noise_edges.at[sender], noise_send.at[k - 1],
            noise_recv.at[sender], {"noise": group, "tile": tile_at(k)},
        )

    def prepare(step, f):
        low_frame = frames_f32[f].astype(BF)
        own_low[step, f] = low_frame
        cut = dot_t(pick[...], low_frame).astype(BF)
        for k in range(1, tiles):
            packs[step, k - 1, f, :, :fields] = cut[(k - 1) * slots : k * slots]

    def send(step, first, last):
        for part in own_parts[step]:
            if first <= part[0] < last:
                for k in range(1, tiles):
                    to_own(step, part, k, me).start()

        @pl.when(group >= 1)
        def _():
            for part in next_parts[step]:
                if first <= part[0] < last:
                    body(step, part).start()
                    for k in range(1, tiles):
                        to_next(step, part, k, me).start()

        if first == 0:
            @pl.when(group >= 2)
            def _():
                front(step).start()
                for k in range(1, tiles):
                    to_second(step, k, me).start()

    def send_first():
        @pl.when(group >= groups - 2)
        def _():
            for k in range(1, tiles):
                to_noise(k, me).start()

        @pl.when(group >= 1)
        def _():
            sigma_copy().start()

        send(0, 0, frame_count)

    def arrive_own(step, f):
        for part in own_parts[step]:
            if part[0] == f:
                for k in range(1, tiles):
                    to_own(step, part, k, tile_at(k)).wait_recv()

    def fill_next(step):
        for s in range(steps):
            next_low[s, 0] = (sigma_own[frame_count - 1 : frame_count] * noise[s]).astype(BF)
            for k in range(1, tiles):
                sender = tile_at(k)
                next_edges[s, sender, 0] = (
                    noise_edges[sender, s].astype(F32) * sigma_own[frame_count - 1 : frame_count, :128]
                ).astype(BF)

    def fill_second():
        for s in range(steps):
            second_low[s] = (sigma_next[frame_count - 1 : frame_count] * noise[s]).astype(BF)
            for k in range(1, tiles):
                sender = tile_at(k)
                second_edges[s, sender] = (
                    noise_edges[sender, s].astype(F32) * sigma_next[frame_count - 1 : frame_count, :128]
                ).astype(BF)

    def arrive_noise():
        @pl.when(group >= groups - 2)
        def _():
            for k in range(1, tiles):
                to_noise(k, tile_at(k)).wait_recv()

        @pl.when(is_last)
        def _():
            fill_next(0)

        @pl.when(group < groups - 1)
        def _():
            sigma_copy().wait_recv()

        @pl.when(is_tail)
        def _():
            fill_second()

    def arrive_next(step, f):
        @pl.when(group < groups - 1)
        def _():
            for part in next_parts[step]:
                if part[0] == f:
                    body(step, part).wait_recv()
                    for k in range(1, tiles):
                        to_next(step, part, k, tile_at(k)).wait_recv()

    def arrive_second(step):
        @pl.when(group < groups - 2)
        def _():
            front(step).wait_recv()
            for k in range(1, tiles):
                to_second(step, k, tile_at(k)).wait_recv()

    def sent():
        for step in range(steps):
            for part in own_parts[step]:
                for k in range(1, tiles):
                    to_own(step, part, k, me).wait_send()

        @pl.when(group >= groups - 2)
        def _():
            for k in range(1, tiles):
                to_noise(k, me).wait_send()

        @pl.when(group >= 1)
        def _():
            sigma_copy().wait_send()
            for step in range(steps):
                for part in next_parts[step]:
                    body(step, part).wait_send()
                    for k in range(1, tiles):
                        to_next(step, part, k, me).wait_send()

        @pl.when(group >= 2)
        def _():
            for step in range(steps):
                front(step).wait_send()
                for k in range(1, tiles):
                    to_second(step, k, me).wait_send()

    def sigma_of(position):
        if position < frame_count:
            return sigma_own[position : position + 1]
        return sigma_next[position - frame_count : position - frame_count + 1]

    def lift(step, position):
        sigma = sigma_of(position)
        in_scale = lax.rsqrt(sigma * sigma + 1.0)
        frame = position + 1
        if frame < frame_count:
            value = frames_f32[frame]
            edges = lambda t: own_edges[step, t, frame].astype(F32)
        elif frame < reach:
            value = next_low[step, frame - frame_count].astype(F32)
            edges = lambda t: next_edges[step, t, frame - frame_count].astype(F32)
            if frame == frame_count:
                entering = sigma_own[frame_count - 1 : frame_count] * noise[step]
                value = jnp.where(is_last, entering, value)
                frames_f32[frame] = value
        else:
            value = second_low[step].astype(F32)
            edges = lambda t: second_edges[step, t].astype(F32)
        scaled[position % 2, :fields] = value * in_scale
        turned = scaled[position % 2].T.astype(BF)
        row = lax.broadcasted_iota(jnp.int32, (side, 1), 0)
        west_rows = east_rows = line_rows = corner_rows = jnp.zeros((side, 128), F32)
        for k in range(1, tiles):
            sender = tile_at(k)
            packet = edges(sender)
            upper, lower = packet[:side], packet[side:]
            west_rows = jnp.where(sender == west, upper, west_rows)
            east_rows = jnp.where(sender == east, lower, east_rows)
            line_rows = jnp.where(sender == above, upper, line_rows)
            corner_rows = jnp.where(
                jnp.logical_and(row == 0, sender == above_west), lower, jnp.where(
                    jnp.logical_and(row == 1, sender == above_east), lower, corner_rows))
        halo = jnp.concatenate([west_rows, east_rows, line_rows, corner_rows], axis=0) * in_scale[:, :128]
        lifted = dot_n(jnp.concatenate([turned, halo.astype(BF)], axis=0), lift_weight[...])
        lifted = lifted + jnp.log(sigma) * level_embed[...]
        lifted = lifted.astype(BF).astype(F32)
        west_col, east_col = lifted[cells : cells + side], lifted[cells + side : cells + 2 * side]
        line = lifted[cells + 2 * side : cells + 3 * side]
        west_end = lifted[cells + 3 * side : cells + 3 * side + 1]
        east_end = lifted[cells + 3 * side + 1 : cells + 3 * side + 2]
        north_row, south_row = jnp.where(has_north, line, 0.0), jnp.where(has_north, 0.0, line)
        tall = jnp.concatenate([north_row, lifted[:cells], south_row], axis=0)
        padded[position, :, width : 2 * width] = tall.astype(BF)

        def spread(end, column):
            rows = [jnp.where(has_north, end, 0.0)] + [column[y : y + 1] for y in range(side)]
            rows.append(jnp.where(has_north, 0.0, end))
            return jnp.concatenate([jnp.broadcast_to(r, (side, width)) for r in rows], axis=0)

        total = (side + 2) * side
        along = lax.broadcasted_iota(jnp.int32, (total, 1), 0) % side
        from_west = jnp.where(along == 0, spread(west_end, west_col), pltpu.roll(tall, 1, 0))
        padded[position, :, :width] = from_west.astype(BF)
        from_east = jnp.where(along == side - 1, spread(east_end, east_col), pltpu.roll(tall, total - 1, 0))
        padded[position, :, 2 * width :] = from_east.astype(BF)

    def convolve(index):
        frames = pl.ds(2 * index, 2)
        total = None
        for offset in range(9):
            down, right = offset // 3, offset % 3
            window = padded[frames, down * side : down * side + cells, right * width : (right + 1) * width]
            product = dot_t(window.reshape(2 * cells, width), conv_weight[offset])
            total = product if total is None else total + product
        centre = padded[frames, side : side + cells, width : 2 * width].reshape(2 * cells, width)
        result = (centre.astype(F32) + total / (1.0 + jnp.exp(-total))).astype(BF)
        hidden[frames] = result.reshape(2, cells, width)
        widened = result.astype(F32)
        mean = jnp.mean(widened * widened, axis=1, keepdims=True)
        norm = (widened * lax.rsqrt(mean + 1e-06) * norm_gain[...]).astype(BF)
        memory[frames] = dot_t(norm, memory_weight[...]).astype(BF).reshape(2, cells, 2 * width)
        normed[frames] = norm.reshape(2, cells, width)

    rows_at_once = cells

    def attend(step, chunk):
        begin = pl.multiple_of(chunk * rows_at_once, rows_at_once)
        here = pl.ds(begin, rows_at_once)
        def partial(i, j):
            product = queries[i, here] * memory[j, here, :width]
            total = product[:, :128]
            for start in range(128, width, 128):
                total = total + product[:, start : start + 128]
            return total

        def score_block(first):
            pieces = [partial(c % frame_count, first + c // frame_count) for c in range(pairs)]
            return dot_n(jnp.concatenate(pieces, axis=1), head_sum[...]) * head_size ** (-0.5)

        near = score_block(0)
        far = jnp.where(is_last, -jnp.inf, score_block(frame_count))
        most = jnp.maximum(near, far)
        most = jnp.maximum(most, pltpu.roll(most, 64, 1))
        most = jnp.maximum(most, pltpu.roll(most, 32, 1))
        near = jnp.exp(near - most)
        far = jnp.exp(far - most)
        total = near + far
        total = total + pltpu.roll(total, 64, 1)
        total = total + pltpu.roll(total, 32, 1)
        inverse = 1.0 / total
        near = (near * inverse).astype(BF)
        far = (far * inverse).astype(BF)
        for i in range(frame_count):
            context = None
            columns = slice(i * frame_count * 128, (i + 1) * frame_count * 128)
            for block, weight in enumerate((near, far)):
                spread = dot_n(weight, head_spread[:, columns]).astype(BF)
                some = None
                for at in range(frame_count):
                    wide = spread[:, at * 128 : (at + 1) * 128]
                    values = memory[block * frame_count + at, here, width:]
                    term = jnp.concatenate([wide] * (width // 128), axis=1) * values
                    some = term if some is None else some + term
                some = some.astype(F32)
                context = some if context is None else context + some
            refined = hidden[i, here].astype(F32) + dot_t(context.astype(BF), attend_out[...])
            projected = dot_t(decode_weight[...], refined.astype(BF))
            sigma = sigma_own[i : i + 1, :rows_at_once]
            spread = sigma * sigma + 1.0
            frame = frames_f32[i + 1, :, here]
            denoised = (1.0 / spread) * frame + (sigma * lax.rsqrt(spread)) * projected
            change = (deltas[i][:, :rows_at_once] - sigma) / sigma
            frames_f32[i, :, here] = frame + change * (frame - denoised)
            if step < steps - 1:
                prepare(step + 1, i)
                send(step + 1, i, i + 1)

    for f in range(frame_count):
        prepare(0, f)
    for s in range(steps):
        cut = dot_t(pick[...], noise[s].astype(BF)).astype(BF)
        for k in range(1, tiles):
            noise_packs[k - 1, s, :, :fields] = cut[(k - 1) * slots : k * slots]
    reached = sum(jnp.where(group - away >= 0, tiles, 0) for away in (1, 2))
    pl.semaphore_wait(barrier, tiles - 1 + reached)
    send_first()
    query_weight[...] = dot_n(order, query_raw[...]).astype(BF)
    memory_weight[:width] = dot_n(order, memory_raw[:width]).astype(BF)
    memory_weight[width:] = dot_n(order, memory_raw[width:]).astype(BF)
    attend_out[...] = dot_t(attend_raw[...], order).astype(BF)
    half = frame_count // 2
    for step in range(steps):
        for position in range(frame_count - 1):
            arrive_own(step, position + 1)
            lift(step, position)
            if position == 1:
                if step == 0:
                    load.wait()
                lax.fori_loop(0, half // 2, lambda index, c: (convolve(index), c)[1], 0)
        if step == 0:
            arrive_noise()
        for position in range(frame_count - 1, reach - 1):
            arrive_next(step, position + 1 - frame_count)
            lift(step, position)
            if position == frame_count - 1:
                lax.fori_loop(half // 2, half, lambda index, c: (convolve(index), c)[1], 0)
        arrive_second(step)
        lift(step, reach - 1)
        lax.fori_loop(half, frame_count, lambda index, c: (convolve(index), c)[1], 0)
        for i in range(frame_count):
            queries[i] = dot_t(normed[i], query_weight[...]).astype(BF)
        lax.fori_loop(0, cells // rows_at_once, lambda chunk, c: (attend(step, chunk), c)[1], 0)
    for half in range(halves):
        across = slice(half * 128, (half + 1) * 128)
        for i in range(frame_count):
            out[pl.ds(i * halves * fields + half, fields, halves), :] = frames_f32[i, :, across]
    sent()


def shards(groups, tiles, queue_state, fresh_noise, plan, levels, neighbours, in_weight, level_embed,
           conv_weight, norm_gain, query_weight, memory_weight, attend_out, decode_weight):
    frames, fields, _, cells = queue_state.shape
    steps = fresh_noise.shape[0]
    width = in_weight.shape[0]
    side = math.isqrt(cells)
    reach = 2 * frames
    slots = 2 * side
    vmem = pl.BlockSpec(memory_space=pltpu.VMEM)
    smem = pl.BlockSpec(memory_space=pltpu.SMEM)
    dma = pltpu.SemaphoreType.DMA
    result = pl.pallas_call(
        functools.partial(kernel, groups, tiles),
        out_shape=jax.ShapeDtypeStruct((frames * fields * cells // 128, 128), F32),
        in_specs=[smem] * 3 + [vmem] * 4 + [pl.BlockSpec(memory_space=pl.ANY)] + [vmem] * 5,
        out_specs=vmem,
        scratch_shapes=[
            pltpu.VMEM(conv_weight.shape, BF),
            pltpu.VMEM(query_weight.shape, BF),
            pltpu.VMEM(memory_weight.shape, BF),
            pltpu.VMEM(attend_out.shape, BF),
            pltpu.VMEM((steps, fields, cells), F32),
            pltpu.VMEM((frames + 1, fields, cells), F32),
            pltpu.VMEM((steps, frames, fields, cells), BF),
            pltpu.VMEM((steps, frames, fields, cells), BF),
            pltpu.VMEM((steps, fields, cells), BF),
            pltpu.VMEM((steps, tiles - 1, frames, slots, 128), BF),
            pltpu.VMEM((steps, tiles, frames, slots, 128), BF),
            pltpu.VMEM((steps, tiles, frames, slots, 128), BF),
            pltpu.VMEM((steps, tiles, slots, 128), BF),
            pltpu.VMEM((tiles - 1, steps, slots, 128), BF),
            pltpu.VMEM((tiles, steps, slots, 128), BF),
            pltpu.VMEM(((tiles - 1) * slots, cells), BF),
            pltpu.VMEM((8, 256), F32),
            pltpu.VMEM((8, 256), F32),
            pltpu.VMEM((128, width), BF),
            pltpu.VMEM((frames * frames * 128, 128), BF),
            pltpu.VMEM((128, frames * frames * 128), BF),
            pltpu.VMEM((2, 128, cells), F32),
            pltpu.VMEM((reach, (side + 2) * side, 3 * width), BF),
            pltpu.VMEM((reach, cells, width), BF),
            pltpu.VMEM((reach, cells, width), BF),
            pltpu.VMEM((frames, cells, width), BF),
            pltpu.VMEM((reach, cells, 2 * width), BF),
            dma,
            dma((steps, frames, tiles - 1)),
            dma((steps, frames, tiles)),
            dma((steps, frames, tiles - 1)),
            dma((steps, frames, tiles)),
            dma((steps, frames)),
            dma((steps, frames)),
            dma((steps, tiles - 1)),
            dma((steps, tiles)),
            dma((tiles - 1,)),
            dma((tiles,)),
            dma((1 + steps,)),
            dma((1 + steps,)),
        ],
        compiler_params=pltpu.CompilerParams(
            collective_id=0, has_side_effects=True, vmem_limit_bytes=56 * 1024 * 1024
        ),
    )(
        levels, plan, neighbours, queue_state.reshape(-1, 128),
        fresh_noise, in_weight.T, level_embed.reshape(1, width),
        conv_weight, norm_gain.reshape(1, width), query_weight, memory_weight, attend_out,
        decode_weight,
    )
    return result.reshape(queue_state.shape)


def solution(mesh):
    body = functools.partial(shards, mesh.shape["noise"], mesh.shape["tile"])
    in_specs = (
        P("noise", None, "tile", None), P(None, None, "tile", None), P(), P("noise"),
    ) + (P(),) * 9
    return jax.shard_map(
        body, mesh=mesh, in_specs=in_specs, out_specs=P("noise", None, "tile", None), check_vma=False
    )
```

```python
import functools
import math

import jax
import jax.numpy as jnp
from jax import lax
from jax.experimental import pallas as pl
from jax.experimental.pallas import tpu as pltpu
from jax.sharding import PartitionSpec as P

HEADS = 8
MESH = pl.DeviceIdType.MESH
BF = jnp.bfloat16
F32 = jnp.float32


def dot_t(left, right):
    return lax.dot_general(left, right, (((1,), (1,)), ((), ())), preferred_element_type=F32)


def dot_n(left, right):
    return lax.dot_general(left, right, (((1,), (0,)), ((), ())), preferred_element_type=F32)


def kernel(
    groups, tiles, levels, plan, neighbours, queue, noise_rows, in_weight, level_embed, conv_hbm,
    norm_gain, query_raw, memory_raw, attend_raw, decode_weight, out,
    conv_weight, query_weight, memory_weight, attend_out, noise, frames_f32, own_low, next_low, second_low,
    packs, own_edges, next_edges, second_edges, noise_packs, noise_edges, pick,
    sigma_own, sigma_next, lift_weight, head_sum, head_spread, scaled,
    padded, hidden, sums, queries, memory, load_sem,
    own_send, own_recv, next_send, next_recv, body_send, body_recv, second_send, second_recv,
    noise_send, noise_recv, single_send, single_recv,
):
    frame_count, fields, cells = padded.shape[0] // 2, in_weight.shape[0], hidden.shape[1]
    steps = own_low.shape[0]
    width = in_weight.shape[1]
    halves = cells // 128
    side = math.isqrt(cells)
    slots = 2 * side
    head_size = width // HEADS
    reach = 2 * frame_count
    me = lax.axis_index("tile")
    group = lax.axis_index("noise")
    is_last = group == groups - 1
    is_tail = group == groups - 2

    def tile_at(k):
        return lax.rem(me + k, tiles)

    load = pltpu.make_async_copy(conv_hbm, conv_weight, load_sem)
    load.start()
    barrier = pltpu.get_barrier_semaphore()
    for k in range(1, tiles):
        pl.semaphore_signal(
            barrier, 1, device_id={"noise": group, "tile": tile_at(k)}, device_id_type=MESH
        )
    for away in (1, 2):
        @pl.when(group + away < groups)
        def _():
            for k in range(tiles):
                pl.semaphore_signal(
                    barrier, 1, device_id={"noise": group + away, "tile": tile_at(k)},
                    device_id_type=MESH,
                )

    def vertical(tile):
        north = neighbours[tile, 2]
        return north >= 0, jnp.maximum(jnp.where(north >= 0, north, neighbours[tile, 3]), 0)

    place = lax.broadcasted_iota(jnp.int32, (slots, cells), 0)
    cell = lax.broadcasted_iota(jnp.int32, (slots, cells), 1)
    for k in range(1, tiles):
        other = tile_at(k)
        up, above = vertical(other)
        base = jnp.where(up, (side - 1) * side, 0)
        target = jnp.where(
            jnp.logical_and(place == side, neighbours[above, 0] == me), base + side - 1,
            jnp.where(jnp.logical_and(place == side + 1, neighbours[above, 1] == me), base, -1))
        target = jnp.where(
            jnp.logical_and(place < side, above == me), base + place, target)
        target = jnp.where(
            jnp.logical_and(place >= side, neighbours[other, 1] == me), (place - side) * side, target)
        target = jnp.where(
            jnp.logical_and(place < side, neighbours[other, 0] == me), place * side + side - 1, target)
        pick[(k - 1) * slots : k * slots] = jnp.where(cell == target, 1.0, 0.0).astype(BF)

    pairs = frame_count * frame_count
    lift_weight[...] = jnp.zeros_like(lift_weight)
    lift_weight[:fields] = in_weight[...]
    scaled[...] = jnp.zeros_like(scaled)
    packs[...] = jnp.zeros_like(packs)
    noise_packs[...] = jnp.zeros_like(noise_packs)
    sigma_own[...] = jnp.ones_like(sigma_own)
    deltas = []
    for i in range(frame_count):
        sigma_own[i : i + 1] = jnp.full((1, 256), plan[levels[i]], F32)
        deltas.append(jnp.full((1, 256), plan[levels[i] + 1], F32))

    @pl.when(is_last)
    def _():
        sigma_next[...] = jnp.ones_like(sigma_next)
        next_low[...] = jnp.zeros_like(next_low)
        next_edges[...] = jnp.zeros_like(next_edges)

    @pl.when(group >= groups - 2)
    def _():
        second_low[...] = jnp.zeros_like(second_low)
        second_edges[...] = jnp.zeros_like(second_edges)

    for half in range(halves):
        across = slice(half * 128, (half + 1) * 128)
        for i in range(frame_count):
            frames_f32[0, i, :, across] = queue[pl.ds(i * halves * fields + half, fields, halves), :]
        for i in range(steps):
            noise[i, :, across] = noise_rows[i, :, 0, across]

    west, east = jnp.maximum(neighbours[me, 0], 0), jnp.maximum(neighbours[me, 1], 0)
    has_north, above = vertical(me)
    above_west = jnp.maximum(neighbours[above, 0], 0)
    above_east = jnp.maximum(neighbours[above, 1], 0)

    def copy(source, target_ref, send, recv, where):
        return pltpu.make_async_remote_copy(
            src_ref=source, dst_ref=target_ref, send_sem=send, recv_sem=recv,
            device_id=where, device_id_type=MESH,
        )

    frame_order = list(range(1, frame_count - 1)) + [0, frame_count - 1]
    single = [(f, f + 1) for f in frame_order]
    next_parts = [[(1, frame_count - 1), (0, 1), (frame_count - 1, frame_count)]] + [single] * (steps - 1)
    own_parts = [[part for part in parts if part[0] > 0] for parts in next_parts]

    def to_own(step, part, k, sender):
        a, b = part
        return copy(
            packs.at[step, k - 1, a:b], own_edges.at[step, sender, a:b], own_send.at[step, a, k - 1],
            own_recv.at[step, a, sender], {"noise": group, "tile": tile_at(k)},
        )

    def to_next(step, part, k, sender):
        a, b = part
        return copy(
            packs.at[step, k - 1, a:b], next_edges.at[step, sender, a:b], next_send.at[step, a, k - 1],
            next_recv.at[step, a, sender], {"noise": group - 1, "tile": tile_at(k)},
        )

    def body(step, part):
        a, b = part
        return copy(
            own_low.at[step, a:b], next_low.at[step, a:b], body_send.at[step, a], body_recv.at[step, a],
            {"noise": group - 1, "tile": me},
        )

    def to_second(step, k, sender):
        return copy(
            packs.at[step, k - 1, 0], second_edges.at[step, sender], second_send.at[step, k - 1],
            second_recv.at[step, sender], {"noise": group - 2, "tile": tile_at(k)},
        )

    def front(step):
        return copy(
            own_low.at[step, 0], second_low.at[step], single_send.at[1 + step], single_recv.at[1 + step],
            {"noise": group - 2, "tile": me},
        )

    def sigma_copy():
        return copy(
            sigma_own, sigma_next, single_send.at[0], single_recv.at[0],
            {"noise": group - 1, "tile": me},
        )

    def to_noise(k, sender):
        return copy(
            noise_packs.at[k - 1], noise_edges.at[sender], noise_send.at[k - 1],
            noise_recv.at[sender], {"noise": group, "tile": tile_at(k)},
        )

    def prepare(step, f):
        low_frame = frames_f32[step % 2, f].astype(BF)
        own_low[step, f] = low_frame
        cut = dot_t(pick[...], low_frame).astype(BF)
        for k in range(1, tiles):
            packs[step, k - 1, f, :, :fields] = cut[(k - 1) * slots : k * slots]

    def send(step, frames):
        for part in own_parts[step]:
            if part[0] in frames:
                for k in range(1, tiles):
                    to_own(step, part, k, me).start()

        @pl.when(group >= 1)
        def _():
            for part in next_parts[step]:
                if part[0] in frames:
                    body(step, part).start()
                    for k in range(1, tiles):
                        to_next(step, part, k, me).start()

        if 0 in frames:
            @pl.when(group >= 2)
            def _():
                front(step).start()
                for k in range(1, tiles):
                    to_second(step, k, me).start()

    def send_first():
        @pl.when(group >= groups - 2)
        def _():
            for k in range(1, tiles):
                to_noise(k, me).start()

        @pl.when(group >= 1)
        def _():
            sigma_copy().start()

        send(0, frame_order)

    def arrive_own(step, f):
        for part in own_parts[step]:
            if part[0] == f:
                for k in range(1, tiles):
                    to_own(step, part, k, tile_at(k)).wait_recv()

    def fill_next(step):
        for s in range(steps):
            next_low[s, 0] = (sigma_own[frame_count - 1 : frame_count] * noise[s]).astype(BF)
            for k in range(1, tiles):
                sender = tile_at(k)
                next_edges[s, sender, 0] = (
                    noise_edges[sender, s].astype(F32) * sigma_own[frame_count - 1 : frame_count, :128]
                ).astype(BF)

    def fill_second():
        for s in range(steps):
            second_low[s] = (sigma_next[frame_count - 1 : frame_count] * noise[s]).astype(BF)
            for k in range(1, tiles):
                sender = tile_at(k)
                second_edges[s, sender] = (
                    noise_edges[sender, s].astype(F32) * sigma_next[frame_count - 1 : frame_count, :128]
                ).astype(BF)

    def arrive_noise():
        @pl.when(group >= groups - 2)
        def _():
            for k in range(1, tiles):
                to_noise(k, tile_at(k)).wait_recv()

        @pl.when(is_last)
        def _():
            fill_next(0)

        @pl.when(group < groups - 1)
        def _():
            sigma_copy().wait_recv()

        @pl.when(is_tail)
        def _():
            fill_second()

    def arrive_next(step, f):
        @pl.when(group < groups - 1)
        def _():
            for part in next_parts[step]:
                if part[0] == f:
                    body(step, part).wait_recv()
                    for k in range(1, tiles):
                        to_next(step, part, k, tile_at(k)).wait_recv()

    def arrive_second(step):
        @pl.when(group < groups - 2)
        def _():
            front(step).wait_recv()
            for k in range(1, tiles):
                to_second(step, k, tile_at(k)).wait_recv()

    def sent():
        for step in range(steps):
            for part in own_parts[step]:
                for k in range(1, tiles):
                    to_own(step, part, k, me).wait_send()

        @pl.when(group >= groups - 2)
        def _():
            for k in range(1, tiles):
                to_noise(k, me).wait_send()

        @pl.when(group >= 1)
        def _():
            sigma_copy().wait_send()
            for step in range(steps):
                for part in next_parts[step]:
                    body(step, part).wait_send()
                    for k in range(1, tiles):
                        to_next(step, part, k, me).wait_send()

        @pl.when(group >= 2)
        def _():
            for step in range(steps):
                front(step).wait_send()
                for k in range(1, tiles):
                    to_second(step, k, me).wait_send()

    def sigma_of(position):
        if position < frame_count:
            return sigma_own[position : position + 1]
        return sigma_next[position - frame_count : position - frame_count + 1]

    def lift(step, position):
        sigma = sigma_of(position)
        in_scale = lax.rsqrt(sigma * sigma + 1.0)
        frame = position + 1
        if frame < frame_count:
            value = frames_f32[step % 2, frame]
            edges = lambda t: own_edges[step, t, frame].astype(F32)
        elif frame < reach:
            value = next_low[step, frame - frame_count].astype(F32)
            edges = lambda t: next_edges[step, t, frame - frame_count].astype(F32)
            if frame == frame_count:
                entering = sigma_own[frame_count - 1 : frame_count] * noise[step]
                value = jnp.where(is_last, entering, value)
                frames_f32[step % 2, frame] = value
        else:
            value = second_low[step].astype(F32)
            edges = lambda t: second_edges[step, t].astype(F32)
        scaled[position % 2, :fields] = value * in_scale
        turned = scaled[position % 2].T.astype(BF)
        row = lax.broadcasted_iota(jnp.int32, (side, 1), 0)
        west_rows = east_rows = line_rows = corner_rows = jnp.zeros((side, 128), F32)
        for k in range(1, tiles):
            sender = tile_at(k)
            packet = edges(sender)
            upper, lower = packet[:side], packet[side:]
            west_rows = jnp.where(sender == west, upper, west_rows)
            east_rows = jnp.where(sender == east, lower, east_rows)
            line_rows = jnp.where(sender == above, upper, line_rows)
            corner_rows = jnp.where(
                jnp.logical_and(row == 0, sender == above_west), lower, jnp.where(
                    jnp.logical_and(row == 1, sender == above_east), lower, corner_rows))
        halo = jnp.concatenate([west_rows, east_rows, line_rows, corner_rows], axis=0) * in_scale[:, :128]
        lifted = dot_n(jnp.concatenate([turned, halo.astype(BF)], axis=0), lift_weight[...])
        lifted = lifted + jnp.log(sigma) * level_embed[...]
        lifted = lifted.astype(BF).astype(F32)
        west_col, east_col = lifted[cells : cells + side], lifted[cells + side : cells + 2 * side]
        line = lifted[cells + 2 * side : cells + 3 * side]
        west_end = lifted[cells + 3 * side : cells + 3 * side + 1]
        east_end = lifted[cells + 3 * side + 1 : cells + 3 * side + 2]
        north_row, south_row = jnp.where(has_north, line, 0.0), jnp.where(has_north, 0.0, line)
        tall = jnp.concatenate([north_row, lifted[:cells], south_row], axis=0)
        padded[position, :, width : 2 * width] = tall.astype(BF)

        def spread(end, column):
            rows = [jnp.where(has_north, end, 0.0)] + [column[y : y + 1] for y in range(side)]
            rows.append(jnp.where(has_north, 0.0, end))
            return jnp.concatenate([jnp.broadcast_to(r, (side, width)) for r in rows], axis=0)

        total = (side + 2) * side
        along = lax.broadcasted_iota(jnp.int32, (total, 1), 0) % side
        from_west = jnp.where(along == 0, spread(west_end, west_col), pltpu.roll(tall, 1, 0))
        padded[position, :, :width] = from_west.astype(BF)
        from_east = jnp.where(along == side - 1, spread(east_end, east_col), pltpu.roll(tall, total - 1, 0))
        padded[position, :, 2 * width :] = from_east.astype(BF)

    def convolve(at, batch):
        frames = slice(2 * batch, 2 * batch + 2)
        total = None
        for offset in range(9):
            down, right = offset // 3, offset % 3
            window = padded[frames, down * side : down * side + cells, right * width : (right + 1) * width]
            product = dot_t(window.reshape(2 * cells, width), conv_weight[offset])
            total = product if total is None else total + product
        sums[at % 2] = total

    def features(at, batch):
        frames = slice(2 * batch, 2 * batch + 2)
        total = sums[at % 2]
        centre = padded[frames, side : side + cells, width : 2 * width].reshape(2 * cells, width)
        result = (centre.astype(F32) + total / (1.0 + jnp.exp(-total))).astype(BF)
        hidden[frames] = result.reshape(2, cells, width)
        widened = result.astype(F32)
        mean = jnp.mean(widened * widened, axis=1, keepdims=True)
        norm = (widened * lax.rsqrt(mean + 1e-06) * norm_gain[...]).astype(BF)
        memory[frames] = dot_t(norm, memory_weight[...]).astype(BF).reshape(2, cells, 2 * width)
        if 2 * batch < frame_count:
            queries[frames] = dot_t(norm, query_weight[...]).astype(BF).reshape(2, cells, width)

    rows_at_once = cells

    def attend(step, chunk):
        begin = pl.multiple_of(chunk * rows_at_once, rows_at_once)
        here = pl.ds(begin, rows_at_once)
        def partial(i, j):
            product = queries[i, here] * memory[j, here, :width]
            total = product[:, :128]
            for start in range(128, width, 128):
                total = total + product[:, start : start + 128]
            return total

        def score_block(first):
            pieces = [partial(c % frame_count, first + c // frame_count) for c in range(pairs)]
            return dot_n(jnp.concatenate(pieces, axis=1), head_sum[...]) * head_size ** (-0.5)

        near = score_block(0)
        far = jnp.where(is_last, -jnp.inf, score_block(frame_count))
        most = jnp.maximum(near, far)
        most = jnp.maximum(most, pltpu.roll(most, 64, 1))
        most = jnp.maximum(most, pltpu.roll(most, 32, 1))
        near = jnp.exp(near - most)
        far = jnp.exp(far - most)
        total = near + far
        total = total + pltpu.roll(total, 64, 1)
        total = total + pltpu.roll(total, 32, 1)
        inverse = 1.0 / total
        near = (near * inverse).astype(BF)
        far = (far * inverse).astype(BF)
        for i in frame_order:
            context = None
            columns = slice(i * frame_count * 128, (i + 1) * frame_count * 128)
            for block, weight in enumerate((near, far)):
                spread = dot_n(weight, head_spread[:, columns]).astype(BF)
                some = None
                for at in range(frame_count):
                    wide = spread[:, at * 128 : (at + 1) * 128]
                    values = memory[block * frame_count + at, here, width:]
                    term = jnp.concatenate([wide] * (width // 128), axis=1) * values
                    some = term if some is None else some + term
                some = some.astype(F32)
                context = some if context is None else context + some
            refined = hidden[i, here].astype(F32) + dot_t(context.astype(BF), attend_out[...])
            projected = dot_t(decode_weight[...], refined.astype(BF))
            sigma = sigma_own[i : i + 1, :rows_at_once]
            spread = sigma * sigma + 1.0
            frame = frames_f32[step % 2, i + 1, :, here]
            denoised = (1.0 / spread) * frame + (sigma * lax.rsqrt(spread)) * projected
            change = (deltas[i][:, :rows_at_once] - sigma) / sigma
            frames_f32[(step + 1) % 2, i, :, here] = frame + change * (frame - denoised)
            if step < steps - 1:
                prepare(step + 1, i)
                send(step + 1, [i])

    for f in range(frame_count):
        prepare(0, f)
    for s in range(steps):
        cut = dot_t(pick[...], noise[s].astype(BF)).astype(BF)
        for k in range(1, tiles):
            noise_packs[k - 1, s, :, :fields] = cut[(k - 1) * slots : k * slots]
    reached = sum(jnp.where(group - away >= 0, tiles, 0) for away in (1, 2))
    pl.semaphore_wait(barrier, tiles - 1 + reached)
    send_first()
    source = lax.broadcasted_iota(jnp.int32, (pairs * 128, 128), 0)
    target = lax.broadcasted_iota(jnp.int32, (pairs * 128, 128), 1)
    low = source % 128
    combo = source // 128
    head_sum[...] = jnp.where(target == combo * HEADS + low % HEADS, 1.0, 0.0).astype(BF)
    source = lax.broadcasted_iota(jnp.int32, (128, pairs * 128), 0)
    target = lax.broadcasted_iota(jnp.int32, (128, pairs * 128), 1)
    place = target // 128
    combo = place % frame_count * frame_count + place // frame_count
    head_spread[...] = jnp.where(source == combo * HEADS + target % HEADS, 1.0, 0.0).astype(BF)
    source = lax.broadcasted_iota(jnp.int32, (width, width), 1)
    target = lax.broadcasted_iota(jnp.int32, (width, width), 0)
    order = jnp.where(
        source == target % HEADS * head_size + target // HEADS, 1.0, 0.0
    ).astype(BF)
    query_weight[...] = dot_n(order, query_raw[...]).astype(BF)
    memory_weight[:width] = dot_n(order, memory_raw[:width]).astype(BF)
    memory_weight[width:] = dot_n(order, memory_raw[width:]).astype(BF)
    attend_out[...] = dot_t(attend_raw[...], order).astype(BF)
    half = frame_count // 2
    batches = list(range(half - 1)) + list(range(half, frame_count - 1)) + [half - 1, frame_count - 1]
    for step in range(steps):
        for at in range(frame_count + 1):
            if at < frame_count:
                batch = batches[at]
                for position in (2 * batch, 2 * batch + 1):
                    if position < frame_count - 1:
                        arrive_own(step, position + 1)
                    elif position < reach - 1:
                        if step == 0 and at == 1 and position == 2 * batch:
                            arrive_noise()
                        arrive_next(step, position + 1 - frame_count)
                    else:
                        arrive_second(step)
                if step == 0 and at == 1:
                    load.wait()
                for position in (2 * batch, 2 * batch + 1):
                    lift(step, position)
            if at >= 1:
                convolve(at - 1, batches[at - 1])
            if at >= 2:
                features(at - 2, batches[at - 2])
        features(frame_count - 1, batches[frame_count - 1])
        lax.fori_loop(0, cells // rows_at_once, lambda chunk, c: (attend(step, chunk), c)[1], 0)
    for half in range(halves):
        across = slice(half * 128, (half + 1) * 128)
        for i in range(frame_count):
            out[pl.ds(i * halves * fields + half, fields, halves), :] = frames_f32[steps % 2, i, :, across]
    sent()


def shards(groups, tiles, queue_state, fresh_noise, plan, levels, neighbours, in_weight, level_embed,
           conv_weight, norm_gain, query_weight, memory_weight, attend_out, decode_weight):
    frames, fields, _, cells = queue_state.shape
    steps = fresh_noise.shape[0]
    width = in_weight.shape[0]
    side = math.isqrt(cells)
    reach = 2 * frames
    slots = 2 * side
    vmem = pl.BlockSpec(memory_space=pltpu.VMEM)
    smem = pl.BlockSpec(memory_space=pltpu.SMEM)
    dma = pltpu.SemaphoreType.DMA
    result = pl.pallas_call(
        functools.partial(kernel, groups, tiles),
        out_shape=jax.ShapeDtypeStruct((frames * fields * cells // 128, 128), F32),
        in_specs=[smem] * 3 + [vmem] * 4 + [pl.BlockSpec(memory_space=pl.ANY)] + [vmem] * 5,
        out_specs=vmem,
        scratch_shapes=[
            pltpu.VMEM(conv_weight.shape, BF),
            pltpu.VMEM(query_weight.shape, BF),
            pltpu.VMEM(memory_weight.shape, BF),
            pltpu.VMEM(attend_out.shape, BF),
            pltpu.VMEM((steps, fields, cells), F32),
            pltpu.VMEM((2, frames + 1, fields, cells), F32),
            pltpu.VMEM((steps, frames, fields, cells), BF),
            pltpu.VMEM((steps, frames, fields, cells), BF),
            pltpu.VMEM((steps, fields, cells), BF),
            pltpu.VMEM((steps, tiles - 1, frames, slots, 128), BF),
            pltpu.VMEM((steps, tiles, frames, slots, 128), BF),
            pltpu.VMEM((steps, tiles, frames, slots, 128), BF),
            pltpu.VMEM((steps, tiles, slots, 128), BF),
            pltpu.VMEM((tiles - 1, steps, slots, 128), BF),
            pltpu.VMEM((tiles, steps, slots, 128), BF),
            pltpu.VMEM(((tiles - 1) * slots, cells), BF),
            pltpu.VMEM((8, 256), F32),
            pltpu.VMEM((8, 256), F32),
            pltpu.VMEM((128, width), BF),
            pltpu.VMEM((frames * frames * 128, 128), BF),
            pltpu.VMEM((128, frames * frames * 128), BF),
            pltpu.VMEM((2, 128, cells), F32),
            pltpu.VMEM((reach, (side + 2) * side, 3 * width), BF),
            pltpu.VMEM((reach, cells, width), BF),
            pltpu.VMEM((2, 2 * cells, width), F32),
            pltpu.VMEM((frames, cells, width), BF),
            pltpu.VMEM((reach, cells, 2 * width), BF),
            dma,
            dma((steps, frames, tiles - 1)),
            dma((steps, frames, tiles)),
            dma((steps, frames, tiles - 1)),
            dma((steps, frames, tiles)),
            dma((steps, frames)),
            dma((steps, frames)),
            dma((steps, tiles - 1)),
            dma((steps, tiles)),
            dma((tiles - 1,)),
            dma((tiles,)),
            dma((1 + steps,)),
            dma((1 + steps,)),
        ],
        compiler_params=pltpu.CompilerParams(
            collective_id=0, has_side_effects=True, vmem_limit_bytes=56 * 1024 * 1024
        ),
    )(
        levels, plan, neighbours, queue_state.reshape(-1, 128),
        fresh_noise, in_weight.T, level_embed.reshape(1, width),
        conv_weight, norm_gain.reshape(1, width), query_weight, memory_weight, attend_out,
        decode_weight,
    )
    return result.reshape(queue_state.shape)


def solution(mesh):
    body = functools.partial(shards, mesh.shape["noise"], mesh.shape["tile"])
    in_specs = (
        P("noise", None, "tile", None), P(None, None, "tile", None), P(), P("noise"),
    ) + (P(),) * 9
    return jax.shard_map(
        body, mesh=mesh, in_specs=in_specs, out_specs=P("noise", None, "tile", None), check_vma=False
    )
```

```python
import functools
import math

import jax
import jax.numpy as jnp
from jax import lax
from jax.experimental import pallas as pl
from jax.experimental.pallas import tpu as pltpu
from jax.sharding import PartitionSpec as P

HEADS = 8
MESH = pl.DeviceIdType.MESH
BF = jnp.bfloat16
F32 = jnp.float32


def dot_t(left, right):
    return lax.dot_general(left, right, (((1,), (1,)), ((), ())), preferred_element_type=F32)


def dot_n(left, right):
    return lax.dot_general(left, right, (((1,), (0,)), ((), ())), preferred_element_type=F32)


def kernel(
    groups, tiles, levels_hbm, plan_hbm, neighbours_hbm, queue_hbm, noise_hbm, in_hbm, embed_hbm, conv_hbm,
    gain_hbm, query_hbm, memory_hbm, attend_hbm, decode_hbm, out,
    levels, plan, neighbours, queue, noise_rows, in_weight, level_embed, norm_gain, query_raw, memory_raw,
    attend_raw, decode_weight, input_sems,
    conv_weight, query_weight, memory_weight, attend_out, noise, frames_f32, own_low, next_low, second_low,
    packs, own_edges, next_edges, second_edges, noise_packs, noise_edges, pick,
    sigma_own, sigma_next, lift_weight, head_sum, head_spread, scaled,
    padded, hidden, sums, queries, memory, load_sem,
    own_send, own_recv, next_send, next_recv, body_send, body_recv, second_send, second_recv,
    noise_send, noise_recv, single_send, single_recv,
):
    frame_count, fields, cells = padded.shape[0] // 2, in_weight.shape[0], hidden.shape[1]
    steps = own_low.shape[0]
    width = in_weight.shape[1]
    halves = cells // 128
    side = math.isqrt(cells)
    slots = 2 * side
    head_size = width // HEADS
    reach = 2 * frame_count
    me = lax.axis_index("tile")
    group = lax.axis_index("noise")
    is_last = group == groups - 1
    is_tail = group == groups - 2

    def tile_at(k):
        return lax.rem(me + k, tiles)

    barrier = pltpu.get_barrier_semaphore()
    for k in range(1, tiles):
        pl.semaphore_signal(
            barrier, 1, device_id={"noise": group, "tile": tile_at(k)}, device_id_type=MESH
        )
    for away in (1, 2):
        @pl.when(group + away < groups)
        def _():
            for k in range(tiles):
                pl.semaphore_signal(
                    barrier, 1, device_id={"noise": group + away, "tile": tile_at(k)},
                    device_id_type=MESH,
                )

    inputs = [pltpu.make_async_copy(*pair, input_sems.at[at]) for at, pair in enumerate((
        (neighbours_hbm, neighbours), (levels_hbm, levels), (plan_hbm, plan), (queue_hbm, queue),
        (noise_hbm, noise_rows), (in_hbm, in_weight), (embed_hbm, level_embed), (gain_hbm, norm_gain),
        (query_hbm, query_raw), (memory_hbm, memory_raw), (attend_hbm, attend_raw), (decode_hbm, decode_weight),
    ))]
    for each in inputs:
        each.start()
    load = pltpu.make_async_copy(conv_hbm, conv_weight, load_sem)
    load.start()
    scaled[...] = jnp.zeros_like(scaled)
    packs[...] = jnp.zeros_like(packs)
    noise_packs[...] = jnp.zeros_like(noise_packs)
    sigma_own[...] = jnp.ones_like(sigma_own)
    lift_weight[...] = jnp.zeros_like(lift_weight)
    @pl.when(is_last)
    def _():
        sigma_next[...] = jnp.ones_like(sigma_next)
        next_low[...] = jnp.zeros_like(next_low)
        next_edges[...] = jnp.zeros_like(next_edges)

    @pl.when(group >= groups - 2)
    def _():
        second_low[...] = jnp.zeros_like(second_low)
        second_edges[...] = jnp.zeros_like(second_edges)

    for each in inputs[:6]:
        each.wait()
    def vertical(tile):
        north = neighbours[tile, 2]
        return north >= 0, jnp.maximum(jnp.where(north >= 0, north, neighbours[tile, 3]), 0)

    place = lax.broadcasted_iota(jnp.int32, (slots, cells), 0)
    cell = lax.broadcasted_iota(jnp.int32, (slots, cells), 1)
    for k in range(1, tiles):
        other = tile_at(k)
        up, above = vertical(other)
        base = jnp.where(up, (side - 1) * side, 0)
        target = jnp.where(
            jnp.logical_and(place == side, neighbours[above, 0] == me), base + side - 1,
            jnp.where(jnp.logical_and(place == side + 1, neighbours[above, 1] == me), base, -1))
        target = jnp.where(
            jnp.logical_and(place < side, above == me), base + place, target)
        target = jnp.where(
            jnp.logical_and(place >= side, neighbours[other, 1] == me), (place - side) * side, target)
        target = jnp.where(
            jnp.logical_and(place < side, neighbours[other, 0] == me), place * side + side - 1, target)
        pick[(k - 1) * slots : k * slots] = jnp.where(cell == target, 1.0, 0.0).astype(BF)

    pairs = frame_count * frame_count
    lift_weight[:fields] = in_weight[...]
    deltas = []
    for i in range(frame_count):
        sigma_own[i : i + 1] = jnp.full((1, 256), plan[levels[i]], F32)
        deltas.append(jnp.full((1, 256), plan[levels[i] + 1], F32))

    for half in range(halves):
        across = slice(half * 128, (half + 1) * 128)
        for i in range(frame_count):
            frames_f32[0, i, :, across] = queue[pl.ds(i * halves * fields + half, fields, halves), :]
        for i in range(steps):
            noise[i, :, across] = noise_rows[i, :, 0, across]

    west, east = jnp.maximum(neighbours[me, 0], 0), jnp.maximum(neighbours[me, 1], 0)
    has_north, above = vertical(me)
    above_west = jnp.maximum(neighbours[above, 0], 0)
    above_east = jnp.maximum(neighbours[above, 1], 0)

    def copy(source, target_ref, send, recv, where):
        return pltpu.make_async_remote_copy(
            src_ref=source, dst_ref=target_ref, send_sem=send, recv_sem=recv,
            device_id=where, device_id_type=MESH,
        )

    frame_order = list(range(1, frame_count - 1)) + [0, frame_count - 1]
    single = [(f, f + 1) for f in frame_order]
    next_parts = [[(1, frame_count - 1), (0, 1), (frame_count - 1, frame_count)]] + [single] * (steps - 1)
    own_parts = [[part for part in parts if part[0] > 0] for parts in next_parts]

    def to_own(step, part, k, sender):
        a, b = part
        return copy(
            packs.at[step, k - 1, a:b], own_edges.at[step, sender, a:b], own_send.at[step, a, k - 1],
            own_recv.at[step, a, sender], {"noise": group, "tile": tile_at(k)},
        )

    def to_next(step, part, k, sender):
        a, b = part
        return copy(
            packs.at[step, k - 1, a:b], next_edges.at[step, sender, a:b], next_send.at[step, a, k - 1],
            next_recv.at[step, a, sender], {"noise": group - 1, "tile": tile_at(k)},
        )

    def body(step, part):
        a, b = part
        return copy(
            own_low.at[step, a:b], next_low.at[step, a:b], body_send.at[step, a], body_recv.at[step, a],
            {"noise": group - 1, "tile": me},
        )

    def to_second(step, k, sender):
        return copy(
            packs.at[step, k - 1, 0], second_edges.at[step, sender], second_send.at[step, k - 1],
            second_recv.at[step, sender], {"noise": group - 2, "tile": tile_at(k)},
        )

    def front(step):
        return copy(
            own_low.at[step, 0], second_low.at[step], single_send.at[1 + step], single_recv.at[1 + step],
            {"noise": group - 2, "tile": me},
        )

    def sigma_copy():
        return copy(
            sigma_own, sigma_next, single_send.at[0], single_recv.at[0],
            {"noise": group - 1, "tile": me},
        )

    def to_noise(k, sender):
        return copy(
            noise_packs.at[k - 1], noise_edges.at[sender], noise_send.at[k - 1],
            noise_recv.at[sender], {"noise": group, "tile": tile_at(k)},
        )

    def prepare(step, f):
        low_frame = frames_f32[step % 2, f].astype(BF)
        own_low[step, f] = low_frame
        cut = dot_t(pick[...], low_frame).astype(BF)
        for k in range(1, tiles):
            packs[step, k - 1, f, :, :fields] = cut[(k - 1) * slots : k * slots]

    def send(step, frames):
        for part in own_parts[step]:
            if part[0] in frames:
                for k in range(1, tiles):
                    to_own(step, part, k, me).start()

        @pl.when(group >= 1)
        def _():
            for part in next_parts[step]:
                if part[0] in frames:
                    body(step, part).start()
                    for k in range(1, tiles):
                        to_next(step, part, k, me).start()

        if 0 in frames:
            @pl.when(group >= 2)
            def _():
                front(step).start()
                for k in range(1, tiles):
                    to_second(step, k, me).start()

    def send_first():
        @pl.when(group >= groups - 2)
        def _():
            for k in range(1, tiles):
                to_noise(k, me).start()

        @pl.when(group >= 1)
        def _():
            sigma_copy().start()

        send(0, frame_order)

    def arrive_own(step, f):
        for part in own_parts[step]:
            if part[0] == f:
                for k in range(1, tiles):
                    to_own(step, part, k, tile_at(k)).wait_recv()

    def fill_next(step):
        for s in range(steps):
            next_low[s, 0] = (sigma_own[frame_count - 1 : frame_count] * noise[s]).astype(BF)
            for k in range(1, tiles):
                sender = tile_at(k)
                next_edges[s, sender, 0] = (
                    noise_edges[sender, s].astype(F32) * sigma_own[frame_count - 1 : frame_count, :128]
                ).astype(BF)

    def fill_second():
        for s in range(steps):
            second_low[s] = (sigma_next[frame_count - 1 : frame_count] * noise[s]).astype(BF)
            for k in range(1, tiles):
                sender = tile_at(k)
                second_edges[s, sender] = (
                    noise_edges[sender, s].astype(F32) * sigma_next[frame_count - 1 : frame_count, :128]
                ).astype(BF)

    def arrive_noise():
        @pl.when(group >= groups - 2)
        def _():
            for k in range(1, tiles):
                to_noise(k, tile_at(k)).wait_recv()

        @pl.when(is_last)
        def _():
            fill_next(0)

        @pl.when(group < groups - 1)
        def _():
            sigma_copy().wait_recv()

        @pl.when(is_tail)
        def _():
            fill_second()

    def arrive_next(step, f):
        @pl.when(group < groups - 1)
        def _():
            for part in next_parts[step]:
                if part[0] == f:
                    body(step, part).wait_recv()
                    for k in range(1, tiles):
                        to_next(step, part, k, tile_at(k)).wait_recv()

    def arrive_second(step):
        @pl.when(group < groups - 2)
        def _():
            front(step).wait_recv()
            for k in range(1, tiles):
                to_second(step, k, tile_at(k)).wait_recv()

    def sent():
        for step in range(steps):
            for part in own_parts[step]:
                for k in range(1, tiles):
                    to_own(step, part, k, me).wait_send()

        @pl.when(group >= groups - 2)
        def _():
            for k in range(1, tiles):
                to_noise(k, me).wait_send()

        @pl.when(group >= 1)
        def _():
            sigma_copy().wait_send()
            for step in range(steps):
                for part in next_parts[step]:
                    body(step, part).wait_send()
                    for k in range(1, tiles):
                        to_next(step, part, k, me).wait_send()

        @pl.when(group >= 2)
        def _():
            for step in range(steps):
                front(step).wait_send()
                for k in range(1, tiles):
                    to_second(step, k, me).wait_send()

    def sigma_of(position):
        if position < frame_count:
            return sigma_own[position : position + 1]
        return sigma_next[position - frame_count : position - frame_count + 1]

    def lift(step, position):
        sigma = sigma_of(position)
        in_scale = lax.rsqrt(sigma * sigma + 1.0)
        frame = position + 1
        if frame < frame_count:
            value = frames_f32[step % 2, frame]
            edges = lambda t: own_edges[step, t, frame].astype(F32)
        elif frame < reach:
            value = next_low[step, frame - frame_count].astype(F32)
            edges = lambda t: next_edges[step, t, frame - frame_count].astype(F32)
            if frame == frame_count:
                entering = sigma_own[frame_count - 1 : frame_count] * noise[step]
                value = jnp.where(is_last, entering, value)
                frames_f32[step % 2, frame] = value
        else:
            value = second_low[step].astype(F32)
            edges = lambda t: second_edges[step, t].astype(F32)
        scaled[position % 2, :fields] = value * in_scale
        turned = scaled[position % 2].T.astype(BF)
        row = lax.broadcasted_iota(jnp.int32, (side, 1), 0)
        west_rows = east_rows = line_rows = corner_rows = jnp.zeros((side, 128), F32)
        for k in range(1, tiles):
            sender = tile_at(k)
            packet = edges(sender)
            upper, lower = packet[:side], packet[side:]
            west_rows = jnp.where(sender == west, upper, west_rows)
            east_rows = jnp.where(sender == east, lower, east_rows)
            line_rows = jnp.where(sender == above, upper, line_rows)
            corner_rows = jnp.where(
                jnp.logical_and(row == 0, sender == above_west), lower, jnp.where(
                    jnp.logical_and(row == 1, sender == above_east), lower, corner_rows))
        halo = jnp.concatenate([west_rows, east_rows, line_rows, corner_rows], axis=0) * in_scale[:, :128]
        lifted = dot_n(jnp.concatenate([turned, halo.astype(BF)], axis=0), lift_weight[...])
        lifted = lifted + jnp.log(sigma) * level_embed[...]
        lifted = lifted.astype(BF).astype(F32)
        west_col, east_col = lifted[cells : cells + side], lifted[cells + side : cells + 2 * side]
        line = lifted[cells + 2 * side : cells + 3 * side]
        west_end = lifted[cells + 3 * side : cells + 3 * side + 1]
        east_end = lifted[cells + 3 * side + 1 : cells + 3 * side + 2]
        north_row, south_row = jnp.where(has_north, line, 0.0), jnp.where(has_north, 0.0, line)
        tall = jnp.concatenate([north_row, lifted[:cells], south_row], axis=0)
        padded[position, :, width : 2 * width] = tall.astype(BF)

        def spread(end, column):
            rows = [jnp.where(has_north, end, 0.0)] + [column[y : y + 1] for y in range(side)]
            rows.append(jnp.where(has_north, 0.0, end))
            return jnp.concatenate([jnp.broadcast_to(r, (side, width)) for r in rows], axis=0)

        total = (side + 2) * side
        along = lax.broadcasted_iota(jnp.int32, (total, 1), 0) % side
        from_west = jnp.where(along == 0, spread(west_end, west_col), pltpu.roll(tall, 1, 0))
        padded[position, :, :width] = from_west.astype(BF)
        from_east = jnp.where(along == side - 1, spread(east_end, east_col), pltpu.roll(tall, total - 1, 0))
        padded[position, :, 2 * width :] = from_east.astype(BF)

    def convolve(at, batch):
        frames = slice(2 * batch, 2 * batch + 2)
        total = None
        for offset in range(9):
            down, right = offset // 3, offset % 3
            window = padded[frames, down * side : down * side + cells, right * width : (right + 1) * width]
            product = dot_t(window.reshape(2 * cells, width), conv_weight[offset])
            total = product if total is None else total + product
        sums[at % 2] = total

    def features(at, batch):
        frames = slice(2 * batch, 2 * batch + 2)
        total = sums[at % 2]
        centre = padded[frames, side : side + cells, width : 2 * width].reshape(2 * cells, width)
        result = (centre.astype(F32) + total / (1.0 + jnp.exp(-total))).astype(BF)
        hidden[frames] = result.reshape(2, cells, width)
        widened = result.astype(F32)
        mean = jnp.mean(widened * widened, axis=1, keepdims=True)
        norm = (widened * lax.rsqrt(mean + 1e-06) * norm_gain[...]).astype(BF)
        memory[frames] = dot_t(norm, memory_weight[...]).astype(BF).reshape(2, cells, 2 * width)
        if 2 * batch < frame_count:
            queries[frames] = dot_t(norm, query_weight[...]).astype(BF).reshape(2, cells, width)

    rows_at_once = cells

    def attend(step, chunk):
        begin = pl.multiple_of(chunk * rows_at_once, rows_at_once)
        here = pl.ds(begin, rows_at_once)
        def partial(i, j):
            product = queries[i, here] * memory[j, here, :width]
            total = product[:, :128]
            for start in range(128, width, 128):
                total = total + product[:, start : start + 128]
            return total

        def score_block(first):
            pieces = [partial(c % frame_count, first + c // frame_count) for c in range(pairs)]
            return dot_n(jnp.concatenate(pieces, axis=1), head_sum[...]) * head_size ** (-0.5)

        near = score_block(0)
        far = jnp.where(is_last, -jnp.inf, score_block(frame_count))
        most = jnp.maximum(near, far)
        most = jnp.maximum(most, pltpu.roll(most, 64, 1))
        most = jnp.maximum(most, pltpu.roll(most, 32, 1))
        near = jnp.exp(near - most)
        far = jnp.exp(far - most)
        total = near + far
        total = total + pltpu.roll(total, 64, 1)
        total = total + pltpu.roll(total, 32, 1)
        inverse = 1.0 / total
        near = (near * inverse).astype(BF)
        far = (far * inverse).astype(BF)
        for i in frame_order:
            context = None
            columns = slice(i * frame_count * 128, (i + 1) * frame_count * 128)
            for block, weight in enumerate((near, far)):
                spread = dot_n(weight, head_spread[:, columns]).astype(BF)
                some = None
                for at in range(frame_count):
                    wide = spread[:, at * 128 : (at + 1) * 128]
                    values = memory[block * frame_count + at, here, width:]
                    term = jnp.concatenate([wide] * (width // 128), axis=1) * values
                    some = term if some is None else some + term
                some = some.astype(F32)
                context = some if context is None else context + some
            refined = hidden[i, here].astype(F32) + dot_t(context.astype(BF), attend_out[...])
            projected = dot_t(decode_weight[...], refined.astype(BF))
            sigma = sigma_own[i : i + 1, :rows_at_once]
            spread = sigma * sigma + 1.0
            frame = frames_f32[step % 2, i + 1, :, here]
            denoised = (1.0 / spread) * frame + (sigma * lax.rsqrt(spread)) * projected
            change = (deltas[i][:, :rows_at_once] - sigma) / sigma
            frames_f32[(step + 1) % 2, i, :, here] = frame + change * (frame - denoised)
            if step < steps - 1:
                prepare(step + 1, i)
                send(step + 1, [i])

    for f in range(frame_count):
        prepare(0, f)
    for s in range(steps):
        cut = dot_t(pick[...], noise[s].astype(BF)).astype(BF)
        for k in range(1, tiles):
            noise_packs[k - 1, s, :, :fields] = cut[(k - 1) * slots : k * slots]
    reached = sum(jnp.where(group - away >= 0, tiles, 0) for away in (1, 2))
    pl.semaphore_wait(barrier, tiles - 1 + reached)
    send_first()
    source = lax.broadcasted_iota(jnp.int32, (pairs * 128, 128), 0)
    target = lax.broadcasted_iota(jnp.int32, (pairs * 128, 128), 1)
    low = source % 128
    combo = source // 128
    head_sum[...] = jnp.where(target == combo * HEADS + low % HEADS, 1.0, 0.0).astype(BF)
    source = lax.broadcasted_iota(jnp.int32, (128, pairs * 128), 0)
    target = lax.broadcasted_iota(jnp.int32, (128, pairs * 128), 1)
    place = target // 128
    combo = place % frame_count * frame_count + place // frame_count
    head_spread[...] = jnp.where(source == combo * HEADS + target % HEADS, 1.0, 0.0).astype(BF)
    source = lax.broadcasted_iota(jnp.int32, (width, width), 1)
    target = lax.broadcasted_iota(jnp.int32, (width, width), 0)
    order = jnp.where(
        source == target % HEADS * head_size + target // HEADS, 1.0, 0.0
    ).astype(BF)
    for each in inputs[6:]:
        each.wait()
    query_weight[...] = dot_n(order, query_raw[...]).astype(BF)
    memory_weight[:width] = dot_n(order, memory_raw[:width]).astype(BF)
    memory_weight[width:] = dot_n(order, memory_raw[width:]).astype(BF)
    attend_out[...] = dot_t(attend_raw[...], order).astype(BF)
    half = frame_count // 2
    batches = list(range(half - 1)) + list(range(half, frame_count - 1)) + [half - 1, frame_count - 1]
    for step in range(steps):
        for at in range(frame_count + 1):
            if at < frame_count:
                batch = batches[at]
                for position in (2 * batch, 2 * batch + 1):
                    if position < frame_count - 1:
                        arrive_own(step, position + 1)
                    elif position < reach - 1:
                        if step == 0 and at == 1 and position == 2 * batch:
                            arrive_noise()
                        arrive_next(step, position + 1 - frame_count)
                    else:
                        arrive_second(step)
                if step == 0 and at == 0:
                    load.wait()
                for position in (2 * batch, 2 * batch + 1):
                    lift(step, position)
                convolve(at, batch)
            if 1 <= at < frame_count:
                features(at - 1, batches[at - 1])
        features(frame_count - 1, batches[frame_count - 1])
        lax.fori_loop(0, cells // rows_at_once, lambda chunk, c: (attend(step, chunk), c)[1], 0)
    for half in range(halves):
        across = slice(half * 128, (half + 1) * 128)
        for i in range(frame_count):
            out[pl.ds(i * halves * fields + half, fields, halves), :] = frames_f32[steps % 2, i, :, across]
    sent()


def shards(groups, tiles, queue_state, fresh_noise, plan, levels, neighbours, in_weight, level_embed,
           conv_weight, norm_gain, query_weight, memory_weight, attend_out, decode_weight):
    frames, fields, _, cells = queue_state.shape
    steps = fresh_noise.shape[0]
    width = in_weight.shape[0]
    side = math.isqrt(cells)
    reach = 2 * frames
    slots = 2 * side
    vmem = pl.BlockSpec(memory_space=pltpu.VMEM)
    dma = pltpu.SemaphoreType.DMA
    result = pl.pallas_call(
        functools.partial(kernel, groups, tiles),
        out_shape=jax.ShapeDtypeStruct((frames * fields * cells // 128, 128), F32),
        in_specs=[pl.BlockSpec(memory_space=pl.ANY)] * 13,
        out_specs=vmem,
        scratch_shapes=[
            pltpu.SMEM(levels.shape, jnp.int32),
            pltpu.SMEM(plan.shape, F32),
            pltpu.SMEM(neighbours.shape, jnp.int32),
            pltpu.VMEM((frames * fields * cells // 128, 128), F32),
            pltpu.VMEM(fresh_noise.shape, F32),
            pltpu.VMEM((fields, width), BF),
            pltpu.VMEM((1, width), F32),
            pltpu.VMEM((1, width), F32),
            pltpu.VMEM(query_weight.shape, BF),
            pltpu.VMEM(memory_weight.shape, BF),
            pltpu.VMEM(attend_out.shape, BF),
            pltpu.VMEM(decode_weight.shape, BF),
            dma((12,)),
            pltpu.VMEM(conv_weight.shape, BF),
            pltpu.VMEM(query_weight.shape, BF),
            pltpu.VMEM(memory_weight.shape, BF),
            pltpu.VMEM(attend_out.shape, BF),
            pltpu.VMEM((steps, fields, cells), F32),
            pltpu.VMEM((2, frames + 1, fields, cells), F32),
            pltpu.VMEM((steps, frames, fields, cells), BF),
            pltpu.VMEM((steps, frames, fields, cells), BF),
            pltpu.VMEM((steps, fields, cells), BF),
            pltpu.VMEM((steps, tiles - 1, frames, slots, 128), BF),
            pltpu.VMEM((steps, tiles, frames, slots, 128), BF),
            pltpu.VMEM((steps, tiles, frames, slots, 128), BF),
            pltpu.VMEM((steps, tiles, slots, 128), BF),
            pltpu.VMEM((tiles - 1, steps, slots, 128), BF),
            pltpu.VMEM((tiles, steps, slots, 128), BF),
            pltpu.VMEM(((tiles - 1) * slots, cells), BF),
            pltpu.VMEM((8, 256), F32),
            pltpu.VMEM((8, 256), F32),
            pltpu.VMEM((128, width), BF),
            pltpu.VMEM((frames * frames * 128, 128), BF),
            pltpu.VMEM((128, frames * frames * 128), BF),
            pltpu.VMEM((2, 128, cells), F32),
            pltpu.VMEM((reach, (side + 2) * side, 3 * width), BF),
            pltpu.VMEM((reach, cells, width), BF),
            pltpu.VMEM((2, 2 * cells, width), F32),
            pltpu.VMEM((frames, cells, width), BF),
            pltpu.VMEM((reach, cells, 2 * width), BF),
            dma,
            dma((steps, frames, tiles - 1)),
            dma((steps, frames, tiles)),
            dma((steps, frames, tiles - 1)),
            dma((steps, frames, tiles)),
            dma((steps, frames)),
            dma((steps, frames)),
            dma((steps, tiles - 1)),
            dma((steps, tiles)),
            dma((tiles - 1,)),
            dma((tiles,)),
            dma((1 + steps,)),
            dma((1 + steps,)),
        ],
        compiler_params=pltpu.CompilerParams(
            collective_id=0, has_side_effects=True, vmem_limit_bytes=56 * 1024 * 1024
        ),
    )(
        levels, plan, neighbours, queue_state.reshape(-1, 128),
        fresh_noise, in_weight.T, level_embed.reshape(1, width),
        conv_weight, norm_gain.reshape(1, width), query_weight, memory_weight, attend_out,
        decode_weight,
    )
    return result.reshape(queue_state.shape)


def solution(mesh):
    body = functools.partial(shards, mesh.shape["noise"], mesh.shape["tile"])
    in_specs = (
        P("noise", None, "tile", None), P(None, None, "tile", None), P(), P("noise"),
    ) + (P(),) * 9
    return jax.shard_map(
        body, mesh=mesh, in_specs=in_specs, out_specs=P("noise", None, "tile", None), check_vma=False
    )
```

```python
import functools
import math

import jax
import jax.numpy as jnp
from jax import lax
from jax.experimental import pallas as pl
from jax.experimental.pallas import tpu as pltpu
from jax.sharding import PartitionSpec as P

HEADS = 8
MESH = pl.DeviceIdType.MESH
BF = jnp.bfloat16
F32 = jnp.float32


def dot_t(left, right):
    return lax.dot_general(left, right, (((1,), (1,)), ((), ())), preferred_element_type=F32)


def dot_n(left, right):
    return lax.dot_general(left, right, (((1,), (0,)), ((), ())), preferred_element_type=F32)


def kernel(
    groups, tiles, levels_hbm, plan_hbm, neighbours_hbm, queue_hbm, noise_hbm, in_hbm, embed_hbm, conv_hbm,
    gain_hbm, query_hbm, memory_hbm, attend_hbm, decode_hbm, out,
    levels, plan, neighbours, queue, noise_rows, in_weight, level_embed, norm_gain, query_raw, memory_raw,
    attend_raw, decode_weight, input_sems,
    conv_weight, query_weight, memory_weight, attend_out, noise, frames_f32, own_low, next_low, second_low,
    packs, own_edges, next_edges, second_edges, noise_packs, noise_edges, pick,
    sigma_own, sigma_next, lift_weight, head_sum, head_spread, scaled,
    padded, hidden, sums, queries, memory, load_sem,
    own_send, own_recv, next_send, next_recv, body_send, body_recv, second_send, second_recv,
    noise_send, noise_recv, single_send, single_recv,
):
    frame_count, fields, cells = padded.shape[0] // 2, in_weight.shape[0], hidden.shape[1]
    steps = own_low.shape[0]
    width = in_weight.shape[1]
    halves = cells // 128
    side = math.isqrt(cells)
    slots = 2 * side
    head_size = width // HEADS
    reach = 2 * frame_count
    me = lax.axis_index("tile")
    group = lax.axis_index("noise")
    is_last = group == groups - 1
    is_tail = group == groups - 2

    def tile_at(k):
        return lax.rem(me + k, tiles)

    barrier = pltpu.get_barrier_semaphore()
    for k in range(1, tiles):
        pl.semaphore_signal(
            barrier, 1, device_id={"noise": group, "tile": tile_at(k)}, device_id_type=MESH
        )
    for away in (1, 2):
        @pl.when(group + away < groups)
        def _():
            for k in range(tiles):
                pl.semaphore_signal(
                    barrier, 1, device_id={"noise": group + away, "tile": tile_at(k)},
                    device_id_type=MESH,
                )

    inputs = [pltpu.make_async_copy(*pair, input_sems.at[at]) for at, pair in enumerate((
        (neighbours_hbm, neighbours), (levels_hbm, levels), (plan_hbm, plan), (queue_hbm, queue),
        (noise_hbm, noise_rows), (in_hbm, in_weight), (embed_hbm, level_embed), (gain_hbm, norm_gain),
        (query_hbm, query_raw), (memory_hbm, memory_raw), (attend_hbm, attend_raw), (decode_hbm, decode_weight),
    ))]
    for each in inputs:
        each.start()
    load = pltpu.make_async_copy(conv_hbm, conv_weight, load_sem)
    load.start()
    scaled[...] = jnp.zeros_like(scaled)
    packs[...] = jnp.zeros_like(packs)
    noise_packs[...] = jnp.zeros_like(noise_packs)
    sigma_own[...] = jnp.ones_like(sigma_own)
    lift_weight[...] = jnp.zeros_like(lift_weight)
    @pl.when(is_last)
    def _():
        sigma_next[...] = jnp.ones_like(sigma_next)
        next_low[...] = jnp.zeros_like(next_low)
        next_edges[...] = jnp.zeros_like(next_edges)

    @pl.when(group >= groups - 2)
    def _():
        second_low[...] = jnp.zeros_like(second_low)
        second_edges[...] = jnp.zeros_like(second_edges)

    for each in inputs[:6]:
        each.wait()
    def vertical(tile):
        north = neighbours[tile, 2]
        return north >= 0, jnp.maximum(jnp.where(north >= 0, north, neighbours[tile, 3]), 0)

    place = lax.broadcasted_iota(jnp.int32, (slots, cells), 0)
    cell = lax.broadcasted_iota(jnp.int32, (slots, cells), 1)
    for k in range(1, tiles):
        other = tile_at(k)
        up, above = vertical(other)
        base = jnp.where(up, (side - 1) * side, 0)
        target = jnp.where(
            jnp.logical_and(place == side, neighbours[above, 0] == me), base + side - 1,
            jnp.where(jnp.logical_and(place == side + 1, neighbours[above, 1] == me), base, -1))
        target = jnp.where(
            jnp.logical_and(place < side, above == me), base + place, target)
        target = jnp.where(
            jnp.logical_and(place >= side, neighbours[other, 1] == me), (place - side) * side, target)
        target = jnp.where(
            jnp.logical_and(place < side, neighbours[other, 0] == me), place * side + side - 1, target)
        pick[(k - 1) * slots : k * slots] = jnp.where(cell == target, 1.0, 0.0).astype(BF)

    pairs = frame_count * frame_count
    lift_weight[:fields] = in_weight[...]
    deltas = []
    for i in range(frame_count):
        sigma_own[i : i + 1] = jnp.full((1, 256), plan[levels[i]], F32)
        deltas.append(jnp.full((1, 256), plan[levels[i] + 1], F32))

    for half in range(halves):
        across = slice(half * 128, (half + 1) * 128)
        for i in range(frame_count):
            frames_f32[0, i, :, across] = queue[pl.ds(i * halves * fields + half, fields, halves), :]
        for i in range(steps):
            noise[i, :, across] = noise_rows[i, :, 0, across]

    west, east = jnp.maximum(neighbours[me, 0], 0), jnp.maximum(neighbours[me, 1], 0)
    has_north, above = vertical(me)
    above_west = jnp.maximum(neighbours[above, 0], 0)
    above_east = jnp.maximum(neighbours[above, 1], 0)

    def copy(source, target_ref, send, recv, where):
        return pltpu.make_async_remote_copy(
            src_ref=source, dst_ref=target_ref, send_sem=send, recv_sem=recv,
            device_id=where, device_id_type=MESH,
        )

    frame_order = list(range(1, frame_count - 1)) + [0, frame_count - 1]
    single = [(f, f + 1) for f in frame_order]
    next_parts = [[(1, frame_count - 1), (0, 1), (frame_count - 1, frame_count)]] + [single] * (steps - 1)
    own_parts = [[part for part in parts if part[0] > 0] for parts in next_parts]

    def to_own(step, part, k, sender):
        a, b = part
        return copy(
            packs.at[step, k - 1, a:b], own_edges.at[step, sender, a:b], own_send.at[step, a, k - 1],
            own_recv.at[step, a, sender], {"noise": group, "tile": tile_at(k)},
        )

    def to_next(step, part, k, sender):
        a, b = part
        return copy(
            packs.at[step, k - 1, a:b], next_edges.at[step, sender, a:b], next_send.at[step, a, k - 1],
            next_recv.at[step, a, sender], {"noise": group - 1, "tile": tile_at(k)},
        )

    def body(step, part):
        a, b = part
        return copy(
            own_low.at[step, a:b], next_low.at[step, a:b], body_send.at[step, a], body_recv.at[step, a],
            {"noise": group - 1, "tile": me},
        )

    def to_second(step, k, sender):
        return copy(
            packs.at[step, k - 1, 0], second_edges.at[step, sender], second_send.at[step, k - 1],
            second_recv.at[step, sender], {"noise": group - 2, "tile": tile_at(k)},
        )

    def front(step):
        return copy(
            own_low.at[step, 0], second_low.at[step], single_send.at[1 + step], single_recv.at[1 + step],
            {"noise": group - 2, "tile": me},
        )

    def sigma_copy():
        return copy(
            sigma_own, sigma_next, single_send.at[0], single_recv.at[0],
            {"noise": group - 1, "tile": me},
        )

    def to_noise(k, sender):
        return copy(
            noise_packs.at[k - 1], noise_edges.at[sender], noise_send.at[k - 1],
            noise_recv.at[sender], {"noise": group, "tile": tile_at(k)},
        )

    def prepare(step, f):
        low_frame = frames_f32[step % 2, f].astype(BF)
        own_low[step, f] = low_frame
        cut = dot_t(pick[...], low_frame).astype(BF)
        for k in range(1, tiles):
            packs[step, k - 1, f, :, :fields] = cut[(k - 1) * slots : k * slots]

    def send(step, frames):
        for part in own_parts[step]:
            if part[0] in frames:
                for k in range(1, tiles):
                    to_own(step, part, k, me).start()

        @pl.when(group >= 1)
        def _():
            for part in next_parts[step]:
                if part[0] in frames:
                    body(step, part).start()
                    for k in range(1, tiles):
                        to_next(step, part, k, me).start()

        if 0 in frames:
            @pl.when(group >= 2)
            def _():
                front(step).start()
                for k in range(1, tiles):
                    to_second(step, k, me).start()

    def send_first():
        @pl.when(group >= groups - 2)
        def _():
            for k in range(1, tiles):
                to_noise(k, me).start()

        @pl.when(group >= 1)
        def _():
            sigma_copy().start()

        send(0, frame_order)

    def arrive_own(step, f):
        for part in own_parts[step]:
            if part[0] == f:
                for k in range(1, tiles):
                    to_own(step, part, k, tile_at(k)).wait_recv()

    def fill_next(step):
        for s in range(steps):
            next_low[s, 0] = (sigma_own[frame_count - 1 : frame_count] * noise[s]).astype(BF)
            for k in range(1, tiles):
                sender = tile_at(k)
                next_edges[s, sender, 0] = (
                    noise_edges[sender, s].astype(F32) * sigma_own[frame_count - 1 : frame_count, :128]
                ).astype(BF)

    def fill_second():
        for s in range(steps):
            second_low[s] = (sigma_next[frame_count - 1 : frame_count] * noise[s]).astype(BF)
            for k in range(1, tiles):
                sender = tile_at(k)
                second_edges[s, sender] = (
                    noise_edges[sender, s].astype(F32) * sigma_next[frame_count - 1 : frame_count, :128]
                ).astype(BF)

    def arrive_noise():
        @pl.when(group >= groups - 2)
        def _():
            for k in range(1, tiles):
                to_noise(k, tile_at(k)).wait_recv()

        @pl.when(is_last)
        def _():
            fill_next(0)

        @pl.when(group < groups - 1)
        def _():
            sigma_copy().wait_recv()

        @pl.when(is_tail)
        def _():
            fill_second()

    def arrive_next(step, f):
        @pl.when(group < groups - 1)
        def _():
            for part in next_parts[step]:
                if part[0] == f:
                    body(step, part).wait_recv()
                    for k in range(1, tiles):
                        to_next(step, part, k, tile_at(k)).wait_recv()

    def arrive_second(step):
        @pl.when(group < groups - 2)
        def _():
            front(step).wait_recv()
            for k in range(1, tiles):
                to_second(step, k, tile_at(k)).wait_recv()

    def sent():
        for step in range(steps):
            for part in own_parts[step]:
                for k in range(1, tiles):
                    to_own(step, part, k, me).wait_send()

        @pl.when(group >= groups - 2)
        def _():
            for k in range(1, tiles):
                to_noise(k, me).wait_send()

        @pl.when(group >= 1)
        def _():
            sigma_copy().wait_send()
            for step in range(steps):
                for part in next_parts[step]:
                    body(step, part).wait_send()
                    for k in range(1, tiles):
                        to_next(step, part, k, me).wait_send()

        @pl.when(group >= 2)
        def _():
            for step in range(steps):
                front(step).wait_send()
                for k in range(1, tiles):
                    to_second(step, k, me).wait_send()

    def sigma_of(position):
        if position < frame_count:
            return sigma_own[position : position + 1]
        return sigma_next[position - frame_count : position - frame_count + 1]

    def lift(step, position):
        sigma = sigma_of(position)
        in_scale = lax.rsqrt(sigma * sigma + 1.0)
        frame = position + 1
        if frame < frame_count:
            value = frames_f32[step % 2, frame]
            edges = lambda t: own_edges[step, t, frame].astype(F32)
        elif frame < reach:
            value = next_low[step, frame - frame_count].astype(F32)
            edges = lambda t: next_edges[step, t, frame - frame_count].astype(F32)
            if frame == frame_count:
                entering = sigma_own[frame_count - 1 : frame_count] * noise[step]
                value = jnp.where(is_last, entering, value)
                frames_f32[step % 2, frame] = value
        else:
            value = second_low[step].astype(F32)
            edges = lambda t: second_edges[step, t].astype(F32)
        scaled[position % 2, :fields] = value * in_scale
        turned = scaled[position % 2].T.astype(BF)
        row = lax.broadcasted_iota(jnp.int32, (side, 1), 0)
        west_rows = east_rows = line_rows = corner_rows = jnp.zeros((side, 128), F32)
        for k in range(1, tiles):
            sender = tile_at(k)
            packet = edges(sender)
            upper, lower = packet[:side], packet[side:]
            west_rows = jnp.where(sender == west, upper, west_rows)
            east_rows = jnp.where(sender == east, lower, east_rows)
            line_rows = jnp.where(sender == above, upper, line_rows)
            corner_rows = jnp.where(
                jnp.logical_and(row == 0, sender == above_west), lower, jnp.where(
                    jnp.logical_and(row == 1, sender == above_east), lower, corner_rows))
        halo = jnp.concatenate([west_rows, east_rows, line_rows, corner_rows], axis=0) * in_scale[:, :128]
        lifted = dot_n(jnp.concatenate([turned, halo.astype(BF)], axis=0), lift_weight[...])
        lifted = lifted + jnp.log(sigma) * level_embed[...]
        lifted = lifted.astype(BF).astype(F32)
        west_col, east_col = lifted[cells : cells + side], lifted[cells + side : cells + 2 * side]
        line = lifted[cells + 2 * side : cells + 3 * side]
        west_end = lifted[cells + 3 * side : cells + 3 * side + 1]
        east_end = lifted[cells + 3 * side + 1 : cells + 3 * side + 2]
        north_row, south_row = jnp.where(has_north, line, 0.0), jnp.where(has_north, 0.0, line)
        tall = jnp.concatenate([north_row, lifted[:cells], south_row], axis=0)
        padded[position, :, width : 2 * width] = tall.astype(BF)

        def spread(end, column):
            rows = [jnp.where(has_north, end, 0.0)] + [column[y : y + 1] for y in range(side)]
            rows.append(jnp.where(has_north, 0.0, end))
            return jnp.concatenate([jnp.broadcast_to(r, (side, width)) for r in rows], axis=0)

        total = (side + 2) * side
        along = lax.broadcasted_iota(jnp.int32, (total, 1), 0) % side
        from_west = jnp.where(along == 0, spread(west_end, west_col), pltpu.roll(tall, 1, 0))
        padded[position, :, :width] = from_west.astype(BF)
        from_east = jnp.where(along == side - 1, spread(east_end, east_col), pltpu.roll(tall, total - 1, 0))
        padded[position, :, 2 * width :] = from_east.astype(BF)

    def convolve(at, batch):
        frames = slice(2 * batch, 2 * batch + 2)
        total = None
        for offset in range(9):
            down, right = offset // 3, offset % 3
            window = padded[frames, down * side : down * side + cells, right * width : (right + 1) * width]
            product = dot_t(window.reshape(2 * cells, width), conv_weight[offset])
            total = product if total is None else total + product
        sums[at % 2] = total

    def features(at, batch):
        frames = slice(2 * batch, 2 * batch + 2)
        total = sums[at % 2]
        centre = padded[frames, side : side + cells, width : 2 * width].reshape(2 * cells, width)
        result = (centre.astype(F32) + total / (1.0 + jnp.exp(-total))).astype(BF)
        hidden[frames] = result.reshape(2, cells, width)
        widened = result.astype(F32)
        mean = jnp.mean(widened * widened, axis=1, keepdims=True)
        norm = (widened * lax.rsqrt(mean + 1e-06) * norm_gain[...]).astype(BF)
        memory[frames] = dot_t(norm, memory_weight[...]).astype(BF).reshape(2, cells, 2 * width)
        if 2 * batch < frame_count:
            queries[frames] = dot_t(norm, query_weight[...]).astype(BF).reshape(2, cells, width)

    rows_at_once = cells

    def attend(step):
        here = slice(0, rows_at_once)
        def partial(i, j):
            product = queries[i, here] * memory[j, here, :width]
            total = product[:, :128]
            for start in range(128, width, 128):
                total = total + product[:, start : start + 128]
            return total

        def score_block(first):
            pieces = [partial(c % frame_count, first + c // frame_count) for c in range(pairs)]
            return dot_n(jnp.concatenate(pieces, axis=1), head_sum[...]) * head_size ** (-0.5)

        near = score_block(0)
        far = jnp.where(is_last, -jnp.inf, score_block(frame_count))
        most = jnp.maximum(near, far)
        most = jnp.maximum(most, pltpu.roll(most, 64, 1))
        most = jnp.maximum(most, pltpu.roll(most, 32, 1))
        near = jnp.exp(near - most)
        far = jnp.exp(far - most)
        total = near + far
        total = total + pltpu.roll(total, 64, 1)
        total = total + pltpu.roll(total, 32, 1)
        inverse = 1.0 / total
        near = (near * inverse).astype(BF)
        far = (far * inverse).astype(BF)
        for i in frame_order:
            context = None
            columns = slice(i * frame_count * 128, (i + 1) * frame_count * 128)
            for block, weight in enumerate((near, far)):
                spread = dot_n(weight, head_spread[:, columns]).astype(BF)
                some = None
                for at in range(frame_count):
                    wide = spread[:, at * 128 : (at + 1) * 128]
                    values = memory[block * frame_count + at, here, width:]
                    term = jnp.concatenate([wide] * (width // 128), axis=1) * values
                    some = term if some is None else some + term
                some = some.astype(F32)
                context = some if context is None else context + some
            refined = hidden[i, here].astype(F32) + dot_t(context.astype(BF), attend_out[...])
            projected = dot_t(decode_weight[...], refined.astype(BF))
            sigma = sigma_own[i : i + 1, :rows_at_once]
            spread = sigma * sigma + 1.0
            frame = frames_f32[step % 2, i + 1, :, here]
            denoised = (1.0 / spread) * frame + (sigma * lax.rsqrt(spread)) * projected
            change = (deltas[i][:, :rows_at_once] - sigma) / sigma
            after = frame + change * (frame - denoised)
            if step == steps - 1:
                for half in range(halves):
                    out[pl.ds(i * halves * fields + half, fields, halves), :] = after[:, half * 128 : (half + 1) * 128]
            else:
                frames_f32[(step + 1) % 2, i, :, here] = after
            if step < steps - 1:
                prepare(step + 1, i)
                send(step + 1, [i])

    for f in range(frame_count):
        prepare(0, f)
    for s in range(steps):
        cut = dot_t(pick[...], noise[s].astype(BF)).astype(BF)
        for k in range(1, tiles):
            noise_packs[k - 1, s, :, :fields] = cut[(k - 1) * slots : k * slots]
    reached = sum(jnp.where(group - away >= 0, tiles, 0) for away in (1, 2))
    pl.semaphore_wait(barrier, tiles - 1 + reached)
    send_first()
    source = lax.broadcasted_iota(jnp.int32, (pairs * 128, 128), 0)
    target = lax.broadcasted_iota(jnp.int32, (pairs * 128, 128), 1)
    low = source % 128
    combo = source // 128
    head_sum[...] = jnp.where(target == combo * HEADS + low % HEADS, 1.0, 0.0).astype(BF)
    source = lax.broadcasted_iota(jnp.int32, (128, pairs * 128), 0)
    target = lax.broadcasted_iota(jnp.int32, (128, pairs * 128), 1)
    place = target // 128
    combo = place % frame_count * frame_count + place // frame_count
    head_spread[...] = jnp.where(source == combo * HEADS + target % HEADS, 1.0, 0.0).astype(BF)
    source = lax.broadcasted_iota(jnp.int32, (width, width), 1)
    target = lax.broadcasted_iota(jnp.int32, (width, width), 0)
    order = jnp.where(
        source == target % HEADS * head_size + target // HEADS, 1.0, 0.0
    ).astype(BF)
    for each in inputs[6:]:
        each.wait()
    query_weight[...] = dot_n(order, query_raw[...]).astype(BF)
    memory_weight[:width] = dot_n(order, memory_raw[:width]).astype(BF)
    memory_weight[width:] = dot_n(order, memory_raw[width:]).astype(BF)
    attend_out[...] = dot_t(attend_raw[...], order).astype(BF)
    half = frame_count // 2
    batches = list(range(half - 1)) + list(range(half, frame_count - 1)) + [half - 1, frame_count - 1]
    for step in range(steps):
        for at in range(frame_count + 1):
            if at < frame_count:
                batch = batches[at]
                for position in (2 * batch, 2 * batch + 1):
                    if position < frame_count - 1:
                        arrive_own(step, position + 1)
                    elif position < reach - 1:
                        if step == 0 and at == 1 and position == 2 * batch:
                            arrive_noise()
                        arrive_next(step, position + 1 - frame_count)
                    else:
                        arrive_second(step)
                if step == 0 and at == 0:
                    load.wait()
                for position in (2 * batch, 2 * batch + 1):
                    lift(step, position)
                convolve(at, batch)
            if 1 <= at < frame_count:
                features(at - 1, batches[at - 1])
        features(frame_count - 1, batches[frame_count - 1])
        attend(step)
    sent()


def shards(groups, tiles, queue_state, fresh_noise, plan, levels, neighbours, in_weight, level_embed,
           conv_weight, norm_gain, query_weight, memory_weight, attend_out, decode_weight):
    frames, fields, _, cells = queue_state.shape
    steps = fresh_noise.shape[0]
    width = in_weight.shape[0]
    side = math.isqrt(cells)
    reach = 2 * frames
    slots = 2 * side
    vmem = pl.BlockSpec(memory_space=pltpu.VMEM)
    dma = pltpu.SemaphoreType.DMA
    result = pl.pallas_call(
        functools.partial(kernel, groups, tiles),
        out_shape=pltpu.VMEM((frames * fields * cells // 128, 128), F32),
        in_specs=[pl.BlockSpec(memory_space=pl.ANY)] * 13,
        out_specs=vmem,
        scratch_shapes=[
            pltpu.SMEM(levels.shape, jnp.int32),
            pltpu.SMEM(plan.shape, F32),
            pltpu.SMEM(neighbours.shape, jnp.int32),
            pltpu.VMEM((frames * fields * cells // 128, 128), F32),
            pltpu.VMEM(fresh_noise.shape, F32),
            pltpu.VMEM((fields, width), BF),
            pltpu.VMEM((1, width), F32),
            pltpu.VMEM((1, width), F32),
            pltpu.VMEM(query_weight.shape, BF),
            pltpu.VMEM(memory_weight.shape, BF),
            pltpu.VMEM(attend_out.shape, BF),
            pltpu.VMEM(decode_weight.shape, BF),
            dma((12,)),
            pltpu.VMEM(conv_weight.shape, BF),
            pltpu.VMEM(query_weight.shape, BF),
            pltpu.VMEM(memory_weight.shape, BF),
            pltpu.VMEM(attend_out.shape, BF),
            pltpu.VMEM((steps, fields, cells), F32),
            pltpu.VMEM((2, frames + 1, fields, cells), F32),
            pltpu.VMEM((steps, frames, fields, cells), BF),
            pltpu.VMEM((steps, frames, fields, cells), BF),
            pltpu.VMEM((steps, fields, cells), BF),
            pltpu.VMEM((steps, tiles - 1, frames, slots, 128), BF),
            pltpu.VMEM((steps, tiles, frames, slots, 128), BF),
            pltpu.VMEM((steps, tiles, frames, slots, 128), BF),
            pltpu.VMEM((steps, tiles, slots, 128), BF),
            pltpu.VMEM((tiles - 1, steps, slots, 128), BF),
            pltpu.VMEM((tiles, steps, slots, 128), BF),
            pltpu.VMEM(((tiles - 1) * slots, cells), BF),
            pltpu.VMEM((8, 256), F32),
            pltpu.VMEM((8, 256), F32),
            pltpu.VMEM((128, width), BF),
            pltpu.VMEM((frames * frames * 128, 128), BF),
            pltpu.VMEM((128, frames * frames * 128), BF),
            pltpu.VMEM((2, 128, cells), F32),
            pltpu.VMEM((reach, (side + 2) * side, 3 * width), BF),
            pltpu.VMEM((reach, cells, width), BF),
            pltpu.VMEM((2, 2 * cells, width), F32),
            pltpu.VMEM((frames, cells, width), BF),
            pltpu.VMEM((reach, cells, 2 * width), BF),
            dma,
            dma((steps, frames, tiles - 1)),
            dma((steps, frames, tiles)),
            dma((steps, frames, tiles - 1)),
            dma((steps, frames, tiles)),
            dma((steps, frames)),
            dma((steps, frames)),
            dma((steps, tiles - 1)),
            dma((steps, tiles)),
            dma((tiles - 1,)),
            dma((tiles,)),
            dma((1 + steps,)),
            dma((1 + steps,)),
        ],
        compiler_params=pltpu.CompilerParams(
            collective_id=0, has_side_effects=True, vmem_limit_bytes=56 * 1024 * 1024
        ),
    )(
        levels, plan, neighbours, queue_state.reshape(-1, 128),
        fresh_noise, in_weight.T, level_embed.reshape(1, width),
        conv_weight, norm_gain.reshape(1, width), query_weight, memory_weight, attend_out,
        decode_weight,
    )
    return result.reshape(queue_state.shape)


def solution(mesh):
    body = functools.partial(shards, mesh.shape["noise"], mesh.shape["tile"])
    in_specs = (
        P("noise", None, "tile", None), P(None, None, "tile", None), P(), P("noise"),
    ) + (P(),) * 9
    return jax.shard_map(
        body, mesh=mesh, in_specs=in_specs, out_specs=P("noise", None, "tile", None), check_vma=False
    )
```

```python
import functools
import math

import jax
import jax.numpy as jnp
from jax import lax
from jax.experimental import pallas as pl
from jax.experimental.pallas import tpu as pltpu
from jax.sharding import PartitionSpec as P

HEADS = 8
MESH = pl.DeviceIdType.MESH
BF = jnp.bfloat16
F32 = jnp.float32


def dot_t(left, right):
    return lax.dot_general(left, right, (((1,), (1,)), ((), ())), preferred_element_type=F32)


def dot_n(left, right):
    return lax.dot_general(left, right, (((1,), (0,)), ((), ())), preferred_element_type=F32)


def kernel(
    groups, tiles, levels_hbm, plan_hbm, neighbours_hbm, queue_hbm, noise_hbm, in_hbm, embed_hbm, conv_hbm,
    gain_hbm, query_hbm, memory_hbm, attend_hbm, decode_hbm, out,
    levels, plan, neighbours, queue, noise_rows, in_weight, level_embed, norm_gain, query_raw, memory_raw,
    attend_raw, decode_weight, input_sems,
    conv_weight, query_weight, memory_weight, attend_out, noise, frames_f32, own_low, next_low, second_low,
    packs, own_edges, next_edges, second_edges, noise_packs, noise_edges, pick,
    sigma_own, sigma_next, lift_weight, head_sum, head_spread, scaled,
    padded, hidden, sums, queries, memory, load_sem,
    own_send, own_recv, next_send, next_recv, body_send, body_recv, second_send, second_recv,
    noise_send, noise_recv, single_send, single_recv,
):
    frame_count, fields, cells = padded.shape[0] // 2, in_weight.shape[0], hidden.shape[1]
    steps = own_low.shape[0]
    width = in_weight.shape[1]
    halves = cells // 128
    side = math.isqrt(cells)
    slots = 2 * side
    head_size = width // HEADS
    reach = 2 * frame_count
    me = lax.axis_index("tile")
    group = lax.axis_index("noise")
    is_last = group == groups - 1
    is_tail = group == groups - 2

    def tile_at(k):
        return lax.rem(me + k, tiles)

    barrier = pltpu.get_barrier_semaphore()
    for k in range(1, tiles):
        pl.semaphore_signal(
            barrier, 1, device_id={"noise": group, "tile": tile_at(k)}, device_id_type=MESH
        )
    for away in (1, 2):
        @pl.when(group + away < groups)
        def _():
            for k in range(tiles):
                pl.semaphore_signal(
                    barrier, 1, device_id={"noise": group + away, "tile": tile_at(k)},
                    device_id_type=MESH,
                )

    inputs = [pltpu.make_async_copy(*pair, input_sems.at[at]) for at, pair in enumerate((
        (neighbours_hbm, neighbours), (levels_hbm, levels), (plan_hbm, plan), (queue_hbm, queue),
        (noise_hbm, noise_rows), (in_hbm, in_weight), (embed_hbm, level_embed), (gain_hbm, norm_gain),
        (query_hbm, query_raw), (memory_hbm, memory_raw), (attend_hbm, attend_raw), (decode_hbm, decode_weight),
    ))]
    for each in inputs:
        each.start()
    load = pltpu.make_async_copy(conv_hbm, conv_weight, load_sem)
    load.start()
    scaled[...] = jnp.zeros_like(scaled)
    packs[...] = jnp.zeros_like(packs)
    noise_packs[...] = jnp.zeros_like(noise_packs)
    sigma_own[...] = jnp.ones_like(sigma_own)
    lift_weight[...] = jnp.zeros_like(lift_weight)
    @pl.when(is_last)
    def _():
        sigma_next[...] = jnp.ones_like(sigma_next)
        next_low[...] = jnp.zeros_like(next_low)
        next_edges[...] = jnp.zeros_like(next_edges)

    @pl.when(group >= groups - 2)
    def _():
        second_low[...] = jnp.zeros_like(second_low)
        second_edges[...] = jnp.zeros_like(second_edges)

    for each in inputs[:6]:
        each.wait()
    def vertical(tile):
        north = neighbours[tile, 2]
        return north >= 0, jnp.maximum(jnp.where(north >= 0, north, neighbours[tile, 3]), 0)

    place = lax.broadcasted_iota(jnp.int32, (slots, cells), 0)
    cell = lax.broadcasted_iota(jnp.int32, (slots, cells), 1)
    for k in range(1, tiles):
        other = tile_at(k)
        up, above = vertical(other)
        base = jnp.where(up, (side - 1) * side, 0)
        target = jnp.where(
            jnp.logical_and(place == side, neighbours[above, 0] == me), base + side - 1,
            jnp.where(jnp.logical_and(place == side + 1, neighbours[above, 1] == me), base, -1))
        target = jnp.where(
            jnp.logical_and(place < side, above == me), base + place, target)
        target = jnp.where(
            jnp.logical_and(place >= side, neighbours[other, 1] == me), (place - side) * side, target)
        target = jnp.where(
            jnp.logical_and(place < side, neighbours[other, 0] == me), place * side + side - 1, target)
        pick[(k - 1) * slots : k * slots] = jnp.where(cell == target, 1.0, 0.0).astype(BF)

    pairs = frame_count * frame_count
    lift_weight[:fields] = in_weight[...]
    deltas = []
    for i in range(frame_count):
        sigma_own[i : i + 1] = jnp.full((1, 256), plan[levels[i]], F32)
        deltas.append(jnp.full((1, 256), plan[levels[i] + 1], F32))

    for half in range(halves):
        across = slice(half * 128, (half + 1) * 128)
        for i in range(frame_count):
            frames_f32[0, i, :, across] = queue[pl.ds(i * halves * fields + half, fields, halves), :]
        for i in range(steps):
            noise[i, :, across] = noise_rows[i, :, 0, across]

    west, east = jnp.maximum(neighbours[me, 0], 0), jnp.maximum(neighbours[me, 1], 0)
    has_north, above = vertical(me)
    above_west = jnp.maximum(neighbours[above, 0], 0)
    above_east = jnp.maximum(neighbours[above, 1], 0)

    def copy(source, target_ref, send, recv, where):
        return pltpu.make_async_remote_copy(
            src_ref=source, dst_ref=target_ref, send_sem=send, recv_sem=recv,
            device_id=where, device_id_type=MESH,
        )

    frame_order = list(range(1, frame_count - 1)) + [0, frame_count - 1]
    single = [(f, f + 1) for f in frame_order]
    next_parts = [[(1, frame_count - 1), (0, 1), (frame_count - 1, frame_count)]] + [single] * (steps - 1)
    own_parts = [[part for part in parts if part[0] > 0] for parts in next_parts]

    def to_own(step, part, k, sender):
        a, b = part
        return copy(
            packs.at[step, k - 1, a:b], own_edges.at[step, sender, a:b], own_send.at[step],
            own_recv.at[step, a, sender], {"noise": group, "tile": tile_at(k)},
        )

    def to_next(step, part, k, sender):
        a, b = part
        return copy(
            packs.at[step, k - 1, a:b], next_edges.at[step, sender, a:b], next_send.at[step],
            next_recv.at[step, a, sender], {"noise": group - 1, "tile": tile_at(k)},
        )

    def body(step, part):
        a, b = part
        return copy(
            own_low.at[step, a:b], next_low.at[step, a:b], body_send.at[step], body_recv.at[step, a],
            {"noise": group - 1, "tile": me},
        )

    def to_second(step, k, sender):
        return copy(
            packs.at[step, k - 1, 0], second_edges.at[step, sender], second_send.at[step],
            second_recv.at[step, sender], {"noise": group - 2, "tile": tile_at(k)},
        )

    def front(step):
        return copy(
            own_low.at[step, 0], second_low.at[step], single_send.at[1 + step], single_recv.at[1 + step],
            {"noise": group - 2, "tile": me},
        )

    def sigma_copy():
        return copy(
            sigma_own, sigma_next, single_send.at[0], single_recv.at[0],
            {"noise": group - 1, "tile": me},
        )

    def to_noise(k, sender):
        return copy(
            noise_packs.at[k - 1], noise_edges.at[sender], noise_send.at[k - 1],
            noise_recv.at[sender], {"noise": group, "tile": tile_at(k)},
        )

    def prepare(step, f):
        low_frame = frames_f32[step % 2, f].astype(BF)
        own_low[step, f] = low_frame
        cut = dot_t(pick[...], low_frame).astype(BF)
        for k in range(1, tiles):
            packs[step, k - 1, f, :, :fields] = cut[(k - 1) * slots : k * slots]

    def send(step, frames):
        for part in own_parts[step]:
            if part[0] in frames:
                for k in range(1, tiles):
                    to_own(step, part, k, me).start()

        @pl.when(group >= 1)
        def _():
            for part in next_parts[step]:
                if part[0] in frames:
                    body(step, part).start()
                    for k in range(1, tiles):
                        to_next(step, part, k, me).start()

        if 0 in frames:
            @pl.when(group >= 2)
            def _():
                front(step).start()
                for k in range(1, tiles):
                    to_second(step, k, me).start()

    def send_first():
        @pl.when(group >= groups - 2)
        def _():
            for k in range(1, tiles):
                to_noise(k, me).start()

        @pl.when(group >= 1)
        def _():
            sigma_copy().start()

        send(0, frame_order)

    def arrive_own(step, f):
        for part in own_parts[step]:
            if part[0] == f:
                for k in range(1, tiles):
                    to_own(step, part, k, tile_at(k)).wait_recv()

    def fill_next(step):
        for s in range(steps):
            next_low[s, 0] = (sigma_own[frame_count - 1 : frame_count] * noise[s]).astype(BF)
            for k in range(1, tiles):
                sender = tile_at(k)
                next_edges[s, sender, 0] = (
                    noise_edges[sender, s].astype(F32) * sigma_own[frame_count - 1 : frame_count, :128]
                ).astype(BF)

    def fill_second():
        for s in range(steps):
            second_low[s] = (sigma_next[frame_count - 1 : frame_count] * noise[s]).astype(BF)
            for k in range(1, tiles):
                sender = tile_at(k)
                second_edges[s, sender] = (
                    noise_edges[sender, s].astype(F32) * sigma_next[frame_count - 1 : frame_count, :128]
                ).astype(BF)

    def arrive_noise():
        @pl.when(group >= groups - 2)
        def _():
            for k in range(1, tiles):
                to_noise(k, tile_at(k)).wait_recv()

        @pl.when(is_last)
        def _():
            fill_next(0)

        @pl.when(group < groups - 1)
        def _():
            sigma_copy().wait_recv()

        @pl.when(is_tail)
        def _():
            fill_second()

    def arrive_next(step, f):
        @pl.when(group < groups - 1)
        def _():
            for part in next_parts[step]:
                if part[0] == f:
                    body(step, part).wait_recv()
                    for k in range(1, tiles):
                        to_next(step, part, k, tile_at(k)).wait_recv()

    def arrive_second(step):
        @pl.when(group < groups - 2)
        def _():
            front(step).wait_recv()
            for k in range(1, tiles):
                to_second(step, k, tile_at(k)).wait_recv()

    def left(source, sem):
        copy(source, source, sem, sem, {"noise": group, "tile": tile_at(1)}).wait_send()

    def sent():
        for step in range(steps):
            left(packs.at[step, :, 1:], own_send.at[step])

        @pl.when(group >= groups - 2)
        def _():
            for k in range(1, tiles):
                to_noise(k, me).wait_send()

        @pl.when(group >= 1)
        def _():
            sigma_copy().wait_send()
            for step in range(steps):
                left(packs.at[step], next_send.at[step])
                left(own_low.at[step], body_send.at[step])

        @pl.when(group >= 2)
        def _():
            for step in range(steps):
                front(step).wait_send()
                left(packs.at[step, :, 0], second_send.at[step])

    def sigma_of(position):
        if position < frame_count:
            return sigma_own[position : position + 1]
        return sigma_next[position - frame_count : position - frame_count + 1]

    def lift(step, position):
        sigma = sigma_of(position)
        in_scale = lax.rsqrt(sigma * sigma + 1.0)
        frame = position + 1
        if frame < frame_count:
            value = frames_f32[step % 2, frame]
            edges = lambda t: own_edges[step, t, frame].astype(F32)
        elif frame < reach:
            value = next_low[step, frame - frame_count].astype(F32)
            edges = lambda t: next_edges[step, t, frame - frame_count].astype(F32)
            if frame == frame_count:
                entering = sigma_own[frame_count - 1 : frame_count] * noise[step]
                value = jnp.where(is_last, entering, value)
                frames_f32[step % 2, frame] = value
        else:
            value = second_low[step].astype(F32)
            edges = lambda t: second_edges[step, t].astype(F32)
        scaled[position % 2, :fields] = value * in_scale
        turned = scaled[position % 2].T.astype(BF)
        row = lax.broadcasted_iota(jnp.int32, (side, 1), 0)
        west_rows = east_rows = line_rows = corner_rows = jnp.zeros((side, 128), F32)
        for k in range(1, tiles):
            sender = tile_at(k)
            packet = edges(sender)
            upper, lower = packet[:side], packet[side:]
            west_rows = jnp.where(sender == west, upper, west_rows)
            east_rows = jnp.where(sender == east, lower, east_rows)
            line_rows = jnp.where(sender == above, upper, line_rows)
            corner_rows = jnp.where(
                jnp.logical_and(row == 0, sender == above_west), lower, jnp.where(
                    jnp.logical_and(row == 1, sender == above_east), lower, corner_rows))
        halo = jnp.concatenate([west_rows, east_rows, line_rows, corner_rows], axis=0) * in_scale[:, :128]
        lifted = dot_n(jnp.concatenate([turned, halo.astype(BF)], axis=0), lift_weight[...])
        lifted = lifted + jnp.log(sigma) * level_embed[...]
        lifted = lifted.astype(BF).astype(F32)
        west_col, east_col = lifted[cells : cells + side], lifted[cells + side : cells + 2 * side]
        line = lifted[cells + 2 * side : cells + 3 * side]
        west_end = lifted[cells + 3 * side : cells + 3 * side + 1]
        east_end = lifted[cells + 3 * side + 1 : cells + 3 * side + 2]
        north_row, south_row = jnp.where(has_north, line, 0.0), jnp.where(has_north, 0.0, line)
        tall = jnp.concatenate([north_row, lifted[:cells], south_row], axis=0)
        padded[position, :, width : 2 * width] = tall.astype(BF)

        def spread(end, column):
            rows = [jnp.where(has_north, end, 0.0)] + [column[y : y + 1] for y in range(side)]
            rows.append(jnp.where(has_north, 0.0, end))
            return jnp.concatenate([jnp.broadcast_to(r, (side, width)) for r in rows], axis=0)

        total = (side + 2) * side
        along = lax.broadcasted_iota(jnp.int32, (total, 1), 0) % side
        from_west = jnp.where(along == 0, spread(west_end, west_col), pltpu.roll(tall, 1, 0))
        padded[position, :, :width] = from_west.astype(BF)
        from_east = jnp.where(along == side - 1, spread(east_end, east_col), pltpu.roll(tall, total - 1, 0))
        padded[position, :, 2 * width :] = from_east.astype(BF)

    def convolve(at, batch):
        frames = slice(2 * batch, 2 * batch + 2)
        total = None
        for offset in range(9):
            down, right = offset // 3, offset % 3
            window = padded[frames, down * side : down * side + cells, right * width : (right + 1) * width]
            product = dot_t(window.reshape(2 * cells, width), conv_weight[offset])
            total = product if total is None else total + product
        sums[at % 2] = total

    def features(at, batch):
        frames = slice(2 * batch, 2 * batch + 2)
        total = sums[at % 2]
        centre = padded[frames, side : side + cells, width : 2 * width].reshape(2 * cells, width)
        result = (centre.astype(F32) + total / (1.0 + jnp.exp(-total))).astype(BF)
        hidden[frames] = result.reshape(2, cells, width)
        widened = result.astype(F32)
        mean = jnp.mean(widened * widened, axis=1, keepdims=True)
        norm = (widened * lax.rsqrt(mean + 1e-06) * norm_gain[...]).astype(BF)
        memory[frames] = dot_t(norm, memory_weight[...]).astype(BF).reshape(2, cells, 2 * width)
        if 2 * batch < frame_count:
            queries[frames] = dot_t(norm, query_weight[...]).astype(BF).reshape(2, cells, width)

    rows_at_once = cells

    def attend(step):
        here = slice(0, rows_at_once)
        def partial(i, j):
            product = queries[i, here] * memory[j, here, :width]
            total = product[:, :128]
            for start in range(128, width, 128):
                total = total + product[:, start : start + 128]
            return total

        def score_block(first):
            pieces = [partial(c % frame_count, first + c // frame_count) for c in range(pairs)]
            return dot_n(jnp.concatenate(pieces, axis=1), head_sum[...]) * head_size ** (-0.5)

        near = score_block(0)
        far = jnp.where(is_last, -jnp.inf, score_block(frame_count))
        most = jnp.maximum(near, far)
        most = jnp.maximum(most, pltpu.roll(most, 64, 1))
        most = jnp.maximum(most, pltpu.roll(most, 32, 1))
        near = jnp.exp(near - most)
        far = jnp.exp(far - most)
        total = near + far
        total = total + pltpu.roll(total, 64, 1)
        total = total + pltpu.roll(total, 32, 1)
        inverse = 1.0 / total
        near = (near * inverse).astype(BF)
        far = (far * inverse).astype(BF)
        for i in frame_order:
            context = None
            columns = slice(i * frame_count * 128, (i + 1) * frame_count * 128)
            for block, weight in enumerate((near, far)):
                spread = dot_n(weight, head_spread[:, columns]).astype(BF)
                some = None
                for at in range(frame_count):
                    wide = spread[:, at * 128 : (at + 1) * 128]
                    values = memory[block * frame_count + at, here, width:]
                    term = jnp.concatenate([wide] * (width // 128), axis=1) * values
                    some = term if some is None else some + term
                some = some.astype(F32)
                context = some if context is None else context + some
            refined = hidden[i, here].astype(F32) + dot_t(context.astype(BF), attend_out[...])
            projected = dot_t(decode_weight[...], refined.astype(BF))
            sigma = sigma_own[i : i + 1, :rows_at_once]
            spread = sigma * sigma + 1.0
            frame = frames_f32[step % 2, i + 1, :, here]
            denoised = (1.0 / spread) * frame + (sigma * lax.rsqrt(spread)) * projected
            change = (deltas[i][:, :rows_at_once] - sigma) / sigma
            after = frame + change * (frame - denoised)
            if step == steps - 1:
                for half in range(halves):
                    out[pl.ds(i * halves * fields + half, fields, halves), :] = after[:, half * 128 : (half + 1) * 128]
            else:
                frames_f32[(step + 1) % 2, i, :, here] = after
            if step < steps - 1:
                prepare(step + 1, i)
                send(step + 1, [i])

    for f in range(frame_count):
        prepare(0, f)
    for s in range(steps):
        cut = dot_t(pick[...], noise[s].astype(BF)).astype(BF)
        for k in range(1, tiles):
            noise_packs[k - 1, s, :, :fields] = cut[(k - 1) * slots : k * slots]
    reached = sum(jnp.where(group - away >= 0, tiles, 0) for away in (1, 2))
    pl.semaphore_wait(barrier, tiles - 1 + reached)
    send_first()
    source = lax.broadcasted_iota(jnp.int32, (pairs * 128, 128), 0)
    target = lax.broadcasted_iota(jnp.int32, (pairs * 128, 128), 1)
    low = source % 128
    combo = source // 128
    head_sum[...] = jnp.where(target == combo * HEADS + low % HEADS, 1.0, 0.0).astype(BF)
    source = lax.broadcasted_iota(jnp.int32, (128, pairs * 128), 0)
    target = lax.broadcasted_iota(jnp.int32, (128, pairs * 128), 1)
    place = target // 128
    combo = place % frame_count * frame_count + place // frame_count
    head_spread[...] = jnp.where(source == combo * HEADS + target % HEADS, 1.0, 0.0).astype(BF)
    source = lax.broadcasted_iota(jnp.int32, (width, width), 1)
    target = lax.broadcasted_iota(jnp.int32, (width, width), 0)
    order = jnp.where(
        source == target % HEADS * head_size + target // HEADS, 1.0, 0.0
    ).astype(BF)
    for each in inputs[6:]:
        each.wait()
    query_weight[...] = dot_n(order, query_raw[...]).astype(BF)
    memory_weight[:width] = dot_n(order, memory_raw[:width]).astype(BF)
    memory_weight[width:] = dot_n(order, memory_raw[width:]).astype(BF)
    attend_out[...] = dot_t(attend_raw[...], order).astype(BF)
    half = frame_count // 2
    batches = list(range(half - 1)) + list(range(half, frame_count - 1)) + [half - 1, frame_count - 1]
    for step in range(steps):
        for at in range(frame_count + 1):
            if at < frame_count:
                batch = batches[at]
                for position in (2 * batch, 2 * batch + 1):
                    if position < frame_count - 1:
                        arrive_own(step, position + 1)
                    elif position < reach - 1:
                        if step == 0 and at == 1 and position == 2 * batch:
                            arrive_noise()
                        arrive_next(step, position + 1 - frame_count)
                    else:
                        arrive_second(step)
                if step == 0 and at == 0:
                    load.wait()
                for position in (2 * batch, 2 * batch + 1):
                    lift(step, position)
                convolve(at, batch)
            if 1 <= at < frame_count:
                features(at - 1, batches[at - 1])
        features(frame_count - 1, batches[frame_count - 1])
        attend(step)
    sent()


def shards(groups, tiles, queue_state, fresh_noise, plan, levels, neighbours, in_weight, level_embed,
           conv_weight, norm_gain, query_weight, memory_weight, attend_out, decode_weight):
    frames, fields, _, cells = queue_state.shape
    steps = fresh_noise.shape[0]
    width = in_weight.shape[0]
    side = math.isqrt(cells)
    reach = 2 * frames
    slots = 2 * side
    vmem = pl.BlockSpec(memory_space=pltpu.VMEM)
    dma = pltpu.SemaphoreType.DMA
    result = pl.pallas_call(
        functools.partial(kernel, groups, tiles),
        out_shape=pltpu.VMEM((frames * fields * cells // 128, 128), F32),
        in_specs=[pl.BlockSpec(memory_space=pl.ANY)] * 13,
        out_specs=vmem,
        scratch_shapes=[
            pltpu.SMEM(levels.shape, jnp.int32),
            pltpu.SMEM(plan.shape, F32),
            pltpu.SMEM(neighbours.shape, jnp.int32),
            pltpu.VMEM((frames * fields * cells // 128, 128), F32),
            pltpu.VMEM(fresh_noise.shape, F32),
            pltpu.VMEM((fields, width), BF),
            pltpu.VMEM((1, width), F32),
            pltpu.VMEM((1, width), F32),
            pltpu.VMEM(query_weight.shape, BF),
            pltpu.VMEM(memory_weight.shape, BF),
            pltpu.VMEM(attend_out.shape, BF),
            pltpu.VMEM(decode_weight.shape, BF),
            dma((12,)),
            pltpu.VMEM(conv_weight.shape, BF),
            pltpu.VMEM(query_weight.shape, BF),
            pltpu.VMEM(memory_weight.shape, BF),
            pltpu.VMEM(attend_out.shape, BF),
            pltpu.VMEM((steps, fields, cells), F32),
            pltpu.VMEM((2, frames + 1, fields, cells), F32),
            pltpu.VMEM((steps, frames, fields, cells), BF),
            pltpu.VMEM((steps, frames, fields, cells), BF),
            pltpu.VMEM((steps, fields, cells), BF),
            pltpu.VMEM((steps, tiles - 1, frames, slots, 128), BF),
            pltpu.VMEM((steps, tiles, frames, slots, 128), BF),
            pltpu.VMEM((steps, tiles, frames, slots, 128), BF),
            pltpu.VMEM((steps, tiles, slots, 128), BF),
            pltpu.VMEM((tiles - 1, steps, slots, 128), BF),
            pltpu.VMEM((tiles, steps, slots, 128), BF),
            pltpu.VMEM(((tiles - 1) * slots, cells), BF),
            pltpu.VMEM((8, 256), F32),
            pltpu.VMEM((8, 256), F32),
            pltpu.VMEM((128, width), BF),
            pltpu.VMEM((frames * frames * 128, 128), BF),
            pltpu.VMEM((128, frames * frames * 128), BF),
            pltpu.VMEM((2, 128, cells), F32),
            pltpu.VMEM((reach, (side + 2) * side, 3 * width), BF),
            pltpu.VMEM((reach, cells, width), BF),
            pltpu.VMEM((2, 2 * cells, width), F32),
            pltpu.VMEM((frames, cells, width), BF),
            pltpu.VMEM((reach, cells, 2 * width), BF),
            dma,
            dma((steps,)),
            dma((steps, frames, tiles)),
            dma((steps,)),
            dma((steps, frames, tiles)),
            dma((steps,)),
            dma((steps, frames)),
            dma((steps,)),
            dma((steps, tiles)),
            dma((tiles - 1,)),
            dma((tiles,)),
            dma((1 + steps,)),
            dma((1 + steps,)),
        ],
        compiler_params=pltpu.CompilerParams(
            collective_id=0, has_side_effects=True, vmem_limit_bytes=56 * 1024 * 1024
        ),
    )(
        levels, plan, neighbours, queue_state.reshape(-1, 128),
        fresh_noise, in_weight.T, level_embed.reshape(1, width),
        conv_weight, norm_gain.reshape(1, width), query_weight, memory_weight, attend_out,
        decode_weight,
    )
    return result.reshape(queue_state.shape)


def solution(mesh):
    body = functools.partial(shards, mesh.shape["noise"], mesh.shape["tile"])
    in_specs = (
        P("noise", None, "tile", None), P(None, None, "tile", None), P(), P("noise"),
    ) + (P(),) * 9
    return jax.shard_map(
        body, mesh=mesh, in_specs=in_specs, out_specs=P("noise", None, "tile", None), check_vma=False
    )
```
